32 devices in a mesh: graph: 8 (over y, x, core), tm: 4 (over z).
Axes of the slice: x: 2, y: 2, z: 4, core: 2. Of those that a mesh axis runs over, the one named last changes fastest.
Arguments:
- series: bfloat16 [16, 32, 4096], P('tm', None, 'graph'), may hold values from -6 to 6
- convolution_weight: bfloat16 [2, 2, 64, 32], replicated, may hold values from -0.75 to 0.75
- convolution_bias: float32 [2, 64], replicated, may hold values from -3 to 3
- mixing_weight: bfloat16 [2, 5, 32, 32], replicated, may hold values from -0.5 to 0.5
- mix_bias: float32 [2, 32], replicated, may hold values from -3 to 3
- tile_values: bfloat16 [32, 3, 128, 128], P('graph'), may hold values from -0.3125 to 0.3125
- tile_cols: int32 [32, 3], P('graph'), may hold values from 0 to 5
- send_index: int32 [8, 8, 32], P('graph'), may hold values from 0 to 511
- send_mask: int32 [8, 8, 32], P('graph'), may hold values 0 or 1
- cotangent: bfloat16 [16, 32, 4096], P('tm', None, 'graph'), may hold values from -6 to 6
Outputs:
- output: bfloat16 [16, 32, 4096], P('tm', None, 'graph')
- grad_series: bfloat16 [16, 32, 4096], P('tm', None, 'graph')
- grad_conv: float32 [2, 2, 64, 32], replicated
- grad_mix: float32 [2, 5, 32, 32], replicated
The draws below stay inside these ranges and needn't reach their ends.
Inputs may be any that keep to these rules, and one draw needn't show every extreme that they name: `send_index`: a local sensor number of the sending partition; a list may name a sensor more than once. `tile_cols`: blocks below 4 are the partition's own sensors, the others its boundary rows.
All inputs are finite; a program needn't handle non-finite values. No bound on the sum of `send_mask` on one device may be relied on, other than what follows from the above.
Results may differ from the reference program's by a relative error of at most 0.0079.
Values may be sent and summed in bfloat16 or wider, within the bound.
A program may use at most 64 MiB of HBM per device.

```python
import math
import jax
import jax.numpy as jnp
from jax import lax

RESIDUAL_WIDTH = 32
DILATION_WIDTH = 32
TILE = 128
TILES_ROW = 3
GATED_LAYERS = 2
HALO = 256
SENS_DEV = 512
SLOTS = 32
ROW_BLOCKS = 4
COL_BLOCKS = 6
TIMES = 16
SENSORS = 4096
N_GRAPH = 8


def plant(entries, own_key, low, largest):
    place = [jax.random.randint(jax.random.fold_in(own_key, axis), (), 0, length) for axis, length in enumerate(entries.shape)]
    widest = entries.shape.index(max(entries.shape))
    beside = place[:widest] + [(place[widest] + 1) % entries.shape[widest]] + place[widest + 1:]
    return entries.at[tuple(place)].set(low).at[tuple(beside)].set(largest)


def steps_of(own_key, extent, pieces, least, high):
    loudness = 1.0
    for axis_at, shards_of in pieces:
        draws = jax.random.uniform(jax.random.fold_in(jax.random.fold_in(own_key, 6), axis_at), (shards_of,), jnp.float32, least / len(pieces), high / len(pieces))
        loudness = loudness * jnp.repeat(jnp.exp(draws), extent[axis_at] // shards_of).reshape((-1,) + (1,) * (len(extent) - 1 - axis_at))
    return loudness


def normal_values(own_key, extent, deviation, bound, pieces=(), kind=jnp.bfloat16):
    factor_of = steps_of(own_key, extent, pieces, -0.22, 0.18) if pieces else 1.0
    values = jax.random.normal(own_key, extent, jnp.float32) * deviation * factor_of
    return jnp.minimum(jnp.maximum(values, -bound), bound).astype(kind)


def setup_inputs(seed: int = 0) -> dict:
    key_of = jax.random.split(jax.random.key(seed), 11)
    series = normal_values(key_of[0], (TIMES, RESIDUAL_WIDTH, SENSORS), 1.0, 6.0, ((0, 4), (2, 8)))
    convolution_weight = normal_values(key_of[1], (GATED_LAYERS, 2, 2 * DILATION_WIDTH, RESIDUAL_WIDTH), (2 * RESIDUAL_WIDTH) ** -0.5, 0.75)
    convolution_bias = normal_values(key_of[2], (GATED_LAYERS, 2 * DILATION_WIDTH), 0.5, 3.0, (), jnp.float32)
    mixing_weight = normal_values(key_of[3], (GATED_LAYERS, 5, RESIDUAL_WIDTH, DILATION_WIDTH), (5 * DILATION_WIDTH) ** -0.5, 0.5)
    mix_bias = normal_values(key_of[4], (GATED_LAYERS, RESIDUAL_WIDTH), 0.5, 3.0, (), jnp.float32)
    tile_values = normal_values(key_of[5], (N_GRAPH * ROW_BLOCKS, TILES_ROW, TILE, TILE), (TILES_ROW * TILE) ** -0.5, 0.3125, ((0, 8),))
    tile_cols = plant(jax.random.randint(key_of[6], (N_GRAPH * ROW_BLOCKS, TILES_ROW), 0, COL_BLOCKS), jax.random.fold_in(key_of[6], 1), 0, COL_BLOCKS - 1).astype(jnp.int32)
    send_index = plant(jax.random.randint(key_of[7], (N_GRAPH, N_GRAPH, SLOTS), 0, SENS_DEV), jax.random.fold_in(key_of[7], 1), 0, SENS_DEV - 1).astype(jnp.int32)
    send_mask = plant((jax.random.randint(key_of[8], (N_GRAPH, N_GRAPH, SLOTS), 0, 4) < 3).astype(jnp.int32), jax.random.fold_in(key_of[8], 1), 0, 1)
    cotangent = normal_values(key_of[9], (TIMES, RESIDUAL_WIDTH, SENSORS), 1.0, 6.0, ((0, 4), (2, 8)))
    return dict(series=series, convolution_weight=convolution_weight, convolution_bias=convolution_bias, mixing_weight=mixing_weight, mix_bias=mix_bias, tile_values=tile_values, tile_cols=tile_cols, send_index=send_index, send_mask=send_mask, cotangent=cotangent)


def apply_tiles(packed):
    extended, columns, values = packed
    height = extended.shape[0]
    blocks = extended.reshape(height, -1, TILE)
    picked = jnp.take(blocks, columns.reshape(-1), axis=1)
    picked = picked.reshape(height, columns.shape[0], columns.shape[1], TILE)
    result = jnp.einsum('mrkj,rkij->mri', picked.astype(jnp.float32), values.astype(jnp.float32))
    return result.reshape(height, -1)

def spread_tiles(packed):
    rows_in, columns, values = packed
    height = rows_in.shape[0]
    blocks = rows_in.reshape(height, columns.shape[0], TILE)
    contrib = jnp.einsum('mri,rkij->rkmj', blocks.astype(jnp.float32), values.astype(jnp.float32))
    contrib = contrib.reshape(-1, height, TILE)
    totals = jax.ops.segment_sum(contrib, columns.reshape(-1).astype(jnp.int32), num_segments=COL_BLOCKS)
    return totals.transpose(1, 0, 2).reshape(height, -1)

def reference(series, convolution_weight, convolution_bias, mixing_weight, mix_bias, tile_values, tile_cols, send_index, send_mask, cotangent):
    part_count = N_GRAPH
    columns = tile_cols.reshape(part_count, ROW_BLOCKS, TILES_ROW)
    values = tile_values.reshape(part_count, ROW_BLOCKS, TILES_ROW, TILE, TILE)
    indices = send_index.reshape(part_count, HALO).astype(jnp.int32)
    live_rows = send_mask.reshape(part_count, HALO).astype(jnp.float32)

    def to_parts(array):
        return array.reshape(TIMES, array.shape[1], part_count, SENS_DEV).transpose(2, 0, 1, 3)

    def from_parts(array):
        return array.transpose(1, 2, 0, 3).reshape(TIMES, array.shape[2], SENSORS)

    def pull(signal):
        height = signal.shape[1] * signal.shape[2]
        flattened = signal.reshape(part_count, height, SENS_DEV)
        picked = jax.vmap(lambda source, rows_at: jnp.take(source, rows_at, axis=1))(flattened, indices)
        outgoing = picked * live_rows[:, None, :].astype(jnp.bfloat16)
        received = outgoing.reshape(part_count, height, part_count, SLOTS).transpose(2, 1, 0, 3).reshape(part_count, height, HALO)
        extended = jnp.concatenate([flattened, received], axis=2)
        result = lax.map(apply_tiles, (extended, columns, values))
        return result.reshape(signal.shape)

    def push(signal):
        height = signal.shape[1] * signal.shape[2]
        flattened = signal.reshape(part_count, height, SENS_DEV)
        totals = lax.map(spread_tiles, (flattened, columns, values))
        local_part = totals[:, :, :SENS_DEV]
        outgoing = totals[:, :, SENS_DEV:].astype(jnp.bfloat16)
        returned = outgoing.reshape(part_count, height, part_count, SLOTS).transpose(2, 1, 0, 3).reshape(part_count, height, HALO)
        addend = returned.astype(jnp.float32) * live_rows[:, None, :]
        local_part = jax.vmap(lambda target, rows_at, extra_rows: target.at[:, rows_at].add(extra_rows))(local_part, indices, addend)
        return local_part.reshape(signal.shape)

    def delayed(signal, shift_by):
        zero_block = jnp.zeros(signal.shape[:1] + (shift_by,) + signal.shape[2:], signal.dtype)
        return jnp.concatenate([zero_block, signal[:, :signal.shape[1] - shift_by]], axis=1)

    def advanced(signal, shift_by):
        zero_block = jnp.zeros(signal.shape[:1] + (shift_by,) + signal.shape[2:], signal.dtype)
        return jnp.concatenate([signal[:, shift_by:], zero_block], axis=1)

    def channel_mix(matrix, signal):
        return jnp.einsum('oc,ptcn->pton', matrix.astype(jnp.float32), signal.astype(jnp.float32))

    def channel_back(matrix, signal):
        return jnp.einsum('oc,pton->ptcn', matrix.astype(jnp.float32), signal.astype(jnp.float32))

    def outer_sum(left_side, right_side):
        return jnp.einsum('pton,ptcn->oc', left_side.astype(jnp.float32), right_side.astype(jnp.float32))
    hidden = to_parts(series)
    saved = []
    for layer_index in range(GATED_LAYERS):
        dilation = layer_index + 1
        lagged = delayed(hidden, dilation)
        preactivation = channel_mix(convolution_weight[layer_index, 0], hidden) + channel_mix(convolution_weight[layer_index, 1], lagged)
        preactivation = preactivation + convolution_bias[layer_index][None, None, :, None]
        filter_half = jnp.tanh(preactivation[:, :, :DILATION_WIDTH])
        gate_half = jax.nn.sigmoid(preactivation[:, :, DILATION_WIDTH:])
        gated = (filter_half * gate_half).astype(jnp.bfloat16)
        fwd_one = pull(gated).astype(jnp.bfloat16)
        back_one = push(gated).astype(jnp.bfloat16)
        fwd_two = pull(fwd_one).astype(jnp.bfloat16)
        back_two = push(back_one).astype(jnp.bfloat16)
        hop_list = (gated, fwd_one, fwd_two, back_one, back_two)
        mixed_sum = mix_bias[layer_index][None, None, :, None] + jnp.zeros((), jnp.float32)
        for hop_order in range(5):
            mixed_sum = mixed_sum + channel_mix(mixing_weight[layer_index, hop_order], hop_list[hop_order])
        saved.append((hidden, lagged, filter_half, gate_half, hop_list))
        hidden = (hidden.astype(jnp.float32) + mixed_sum).astype(jnp.bfloat16)
    output = from_parts(hidden)
    grad_flow = to_parts(cotangent).astype(jnp.float32)
    conv_list = [None] * GATED_LAYERS
    mix_list = [None] * GATED_LAYERS
    for layer_index in reversed(range(GATED_LAYERS)):
        dilation = layer_index + 1
        hidden, lagged, filter_half, gate_half, hop_list = saved[layer_index]
        flow_round = grad_flow.astype(jnp.bfloat16)
        mix_list[layer_index] = jnp.stack([outer_sum(flow_round, hop_list[hop_order]) for hop_order in range(5)])
        hop_grads = [channel_back(mixing_weight[layer_index, hop_order], flow_round) for hop_order in range(5)]
        fwd_inner = push(hop_grads[2].astype(jnp.bfloat16))
        back_inner = pull(hop_grads[4].astype(jnp.bfloat16))
        fwd_outer = push((hop_grads[1] + fwd_inner).astype(jnp.bfloat16))
        back_outer = pull((hop_grads[3] + back_inner).astype(jnp.bfloat16))
        grad_gated = hop_grads[0] + fwd_outer + back_outer
        grad_filter = grad_gated * gate_half * (1.0 - filter_half * filter_half)
        grad_gate = grad_gated * filter_half * gate_half * (1.0 - gate_half)
        grad_pre = jnp.concatenate([grad_filter, grad_gate], axis=2).astype(jnp.bfloat16)
        conv_list[layer_index] = jnp.stack([outer_sum(grad_pre, hidden), outer_sum(grad_pre, lagged)])
        lag_term = channel_back(convolution_weight[layer_index, 1], grad_pre)
        grad_flow = grad_flow + channel_back(convolution_weight[layer_index, 0], grad_pre) + advanced(lag_term, dilation)
    norm_scale = 1.0 / math.sqrt(float(TIMES * SENSORS))
    grad_conv = jnp.stack(conv_list) * norm_scale
    grad_mix = jnp.stack(mix_list) * norm_scale
    return (output, from_parts(grad_flow).astype(jnp.bfloat16), grad_conv, grad_mix)
```

```python
import functools
import math

import jax
import jax.numpy as jnp
from jax import lax
from jax.experimental import pallas as pl
from jax.experimental.pallas import tpu as pltpu
from jax.sharding import PartitionSpec as P

GATED_LAYERS = 2
HOPS = 5
BF = jnp.bfloat16
F32 = jnp.float32
MESH = pl.DeviceIdType.MESH


def dot(a, b):
    return lax.dot_general(a, b, (((1,), (0,)), ((), ())), preferred_element_type=F32)


def dot_nt(a, b):
    return lax.dot_general(a, b, (((1,), (1,)), ((), ())), preferred_element_type=F32)


def dot_tn(a, b):
    return lax.dot_general(a, b, (((0,), (0,)), ((), ())), preferred_element_type=F32)


def peers(count, body):
    if count <= 8:
        for off in range(1, count):
            body(off)
    elif count > 1:
        lax.fori_loop(1, count, lambda off, c: (body(off), c)[1], 0)


def kernel(
    n_graph, n_tm, steps, scale,
    series, cw, cb, mw, mb, tv, tcol, sidx, smask, cot,
    out, gser, gconv, gmix,
    wl, wlt, wh, wht, gm, gmt, band, mixall, ext, hops, filt, gate, flow, ctr,
    prev0, pack_s, pack_r, send, recv, e_buf, et_buf, l_buf, lt_buf,
    r_ssem, r_rsem, t_ssem, t_rsem, e_ssem, e_rsem, et_ssem, et_rsem,
    l_ssem, l_rsem, lt_ssem, lt_rsem,
):
    me = lax.axis_index("graph")
    z = lax.axis_index("tm")
    tc, sensors = series.shape
    ch = tc // steps
    half_s = sensors // 2
    slots = sidx.shape[1]
    halo = n_graph * slots
    tile = tv.shape[-1]
    rblocks, tslots = tcol.shape
    lblocks = sensors // tile
    hblocks = halo // tile
    wire = send.dtype

    barrier = pltpu.get_barrier_semaphore()

    def greet_graph(off):
        pl.semaphore_signal(barrier, inc=1, device_id={"graph": lax.rem(me + off, n_graph)}, device_id_type=MESH)

    def greet_tm(off):
        pl.semaphore_signal(barrier, inc=1, device_id={"tm": lax.rem(z + off, n_tm)}, device_id_type=MESH)

    peers(n_graph, greet_graph)
    peers(n_tm, greet_tm)
    pl.semaphore_wait(barrier, n_graph - 1 + n_tm - 1)

    def shift_copy(slot, src, dst, by):
        return pltpu.make_async_remote_copy(
            src_ref=src, dst_ref=dst, send_sem=t_ssem.at[slot], recv_sem=t_rsem.at[slot],
            device_id={"tm": lax.rem(z + by + n_tm, n_tm)}, device_id_type=MESH,
        )

    up = z < n_tm - 1
    down = z > 0

    first = shift_copy(0, series.at[pl.ds(tc - ch, ch)], prev0.at[pl.ds(tc - ch, ch)], 1)
    prev0[pl.ds(0, tc - ch), :] = jnp.zeros((tc - ch, sensors), BF)

    @pl.when(up)
    def _():
        first.start()

    row32 = lax.broadcasted_iota(jnp.int32, (ch, tc), 0)
    lane32 = lax.broadcasted_iota(jnp.int32, (ch, tc), 1)
    spread = jnp.where(lax.rem(lane32, ch) == row32, 1.0, 0.0)
    spread_b = spread.astype(BF)
    rt = lax.broadcasted_iota(jnp.int32, (tc, tc), 0) // ch
    lt = lax.broadcasted_iota(jnp.int32, (tc, tc), 1) // ch
    same = rt == lt

    def before(d):
        return lt == rt - d

    def before_prev(d):
        return lt == rt - d + steps

    cwr = dot(cw[...], spread_b)
    mwr = dot(mw[...], spread_b)

    def stack(x, base):
        return jnp.concatenate([x[base:base + ch]] * steps, axis=0)

    for l in range(GATED_LAYERS):
        d = l + 1
        for h in range(2):
            w0 = stack(cwr, (l * 2 + 0) * 2 * ch + h * ch)
            w1 = stack(cwr, (l * 2 + 1) * 2 * ch + h * ch)
            own = jnp.where(same, w0, 0.0) + jnp.where(before(d), w1, 0.0)
            band[l, pl.ds(h * tc, tc), pl.ds(0, tc)] = own.astype(BF)
            band[l, pl.ds(h * tc, tc), pl.ds(tc, tc)] = jnp.where(before_prev(d), w1, 0.0).astype(BF)
        for k in range(HOPS):
            mk = stack(mwr, (l * HOPS + k) * ch)
            mixall[l, :, pl.ds(k * tc, tc)] = jnp.where(same, mk, 0.0).astype(BF)

    r64 = lax.broadcasted_iota(jnp.int32, (2 * ch, 2 * tc), 0)
    l64 = lax.broadcasted_iota(jnp.int32, (2 * ch, 2 * tc), 1)
    spread2 = jnp.where(lax.rem(l64, ch) + (l64 // tc) * ch == r64, 1.0, 0.0)
    cbias = lax.dot_general(cb[...], spread2, (((1,), (0,)), ((), ())), precision=lax.Precision.HIGHEST, preferred_element_type=F32)
    mbias = lax.dot_general(mb[...], spread, (((1,), (0,)), ((), ())), precision=lax.Precision.HIGHEST, preferred_element_type=F32)

    for r in range(rblocks):
        tiles = [tv[r * tslots + k].astype(F32) for k in range(tslots)]
        flips = [t.T for t in tiles]
        for c in range(lblocks + hblocks):
            a = jnp.zeros((tile, tile), F32)
            b = jnp.zeros((tile, tile), F32)
            for k in range(tslots):
                on = (tcol[r, k] == c).astype(jnp.int32).astype(F32)
                a = a + tiles[k] * on
                b = b + flips[k] * on
            a = a.astype(BF)
            b = b.astype(BF)
            if c < lblocks:
                wl[pl.ds(r * tile, tile), pl.ds(c * tile, tile)] = a
                wlt[pl.ds(c * tile, tile), pl.ds(r * tile, tile)] = b
            else:
                ch_at = c - lblocks
                wh[pl.ds(r * tile, tile), pl.ds(ch_at * tile, tile)] = a
                wht[pl.ds(ch_at * tile, tile), pl.ds(r * tile, tile)] = b

    key = jnp.where(smask[...] != 0, sidx[...] + 1, 0)
    es = lax.broadcasted_iota(jnp.int32, (slots, halo), 0)
    ej = lax.broadcasted_iota(jnp.int32, (slots, halo), 1)
    pick = jnp.where(lax.rem(ej, slots) == es, 1.0, 0.0).astype(BF)
    hi = dot((key // 32).astype(F32).astype(BF), pick)
    lo = dot(lax.rem(key, 32).astype(F32).astype(BF), pick)
    pr = lax.broadcasted_iota(jnp.int32, (n_graph, halo), 0)
    pj = lax.broadcasted_iota(jnp.int32, (n_graph, halo), 1) // slots
    keys = jnp.sum(jnp.where(pr == pj, hi * 32.0 + lo, 0.0), axis=0, keepdims=True)
    ids = lax.broadcasted_iota(jnp.int32, (sensors, halo), 0).astype(F32) + 1.0
    onehot = jnp.where(ids == keys, 1.0, 0.0)
    gm[...] = onehot.astype(BF)
    gmt[...] = onehot.T.astype(BF)

    ext[0, :, pl.ds(0, tc)] = series[...].astype(F32).T.astype(BF)
    ctr[...] = cot[...].astype(F32).T

    def graph_copy(src, dst, ssem, rsem, p):
        return pltpu.make_async_remote_copy(
            src_ref=src, dst_ref=dst, send_sem=ssem, recv_sem=rsem,
            device_id={"graph": p}, device_id_type=MESH,
        )

    def tm_copy(src, dst, ssem, rsem, p):
        return pltpu.make_async_remote_copy(
            src_ref=src, dst_ref=dst, send_sem=ssem, recv_sem=rsem,
            device_id={"tm": p}, device_id_type=MESH,
        )

    def pair(r, pull_in, push_in, filler):
        sp = dot(gmt[...], pull_in)
        sb = dot(wht[...], push_in).astype(BF).astype(F32)
        send[r, :, 0] = sp.reshape(n_graph, slots, tc).astype(wire)
        send[r, :, 1] = sb.reshape(n_graph, slots, tc).astype(wire)

        def go(off):
            p = lax.rem(me + off, n_graph)
            graph_copy(send.at[r, p], recv.at[r, me], r_ssem.at[r, p], r_rsem.at[r, me], p).start()

        peers(n_graph, go)
        recv[r, me] = send[r, me]
        pulled = dot(wl[...], pull_in)
        pushed = dot(wlt[...], push_in)
        filler()

        def take(off):
            p = lax.rem(me + off, n_graph)
            graph_copy(send.at[r, p], recv.at[r, p], r_ssem.at[r, p], r_rsem.at[r, p], p).wait_recv()

        peers(n_graph, take)
        rp = recv[r, :, 0].astype(F32).reshape(halo, tc).astype(BF)
        rb = recv[r, :, 1].astype(F32).reshape(halo, tc).astype(BF)
        return pulled + dot(wh[...], rp), pushed + dot(gm[...], rb)

    lane_half = lax.broadcasted_iota(jnp.int32, (half_s, tc), 1) < tc // 2

    def pack(x):
        return jnp.where(lane_half, pltpu.roll(x[:half_s], tc // 2, 1), x[half_s:]).astype(BF)

    def unpack(p):
        x = p.astype(F32)
        return jnp.concatenate([pltpu.roll(x, tc // 2, 1), x], axis=0)

    nothing = lambda: None

    for l in range(GATED_LAYERS):
        if l == 0:
            @pl.when(down)
            def _():
                first.wait_recv()

            @pl.when(jnp.logical_not(down))
            def _():
                prev0[pl.ds(tc - ch, ch), :] = jnp.zeros((ch, sensors), BF)

            ext[0, :, pl.ds(tc, tc)] = prev0[...].astype(F32).T.astype(BF)
            pre = dot_nt(ext[0], band[0])
        else:
            pre_own = dot_nt(ext[l, :, pl.ds(0, tc)], band[l, :, pl.ds(0, tc)])

            @pl.when(down)
            def _():
                shift_copy(1, pack_s.at[0], pack_r.at[0], 1).wait_recv()

            @pl.when(jnp.logical_not(down))
            def _():
                pack_r[0] = jnp.zeros((half_s, tc), BF)

            ext[l, :, pl.ds(tc, tc)] = unpack(pack_r[0]).astype(BF)
            pre = pre_own + dot_nt(ext[l, :, pl.ds(tc, tc)], band[l, :, pl.ds(tc, tc)])
        pre = pre + cbias[l:l + 1]
        f = jnp.tanh(pre[:, :tc])
        g = jax.nn.sigmoid(pre[:, tc:])
        filt[l] = f
        gate[l] = g
        gated = (f * g).astype(BF)
        hops[l, :, pl.ds(0, tc)] = gated
        fo, bo = pair(2 * l, gated, gated, nothing)
        fo = fo.astype(BF)
        bo = bo.astype(BF)
        hops[l, :, pl.ds(tc, tc)] = fo
        hops[l, :, pl.ds(3 * tc, tc)] = bo
        part = []

        def mix_early():
            m = dot_nt(hops[l, :, pl.ds(0, 2 * tc)], mixall[l, :, pl.ds(0, 2 * tc)])
            part.append(m + dot_nt(hops[l, :, pl.ds(3 * tc, tc)], mixall[l, :, pl.ds(3 * tc, tc)]))

        f2, b2 = pair(2 * l + 1, fo, bo, mix_early)
        f2 = f2.astype(BF)
        b2 = b2.astype(BF)
        hops[l, :, pl.ds(2 * tc, tc)] = f2
        hops[l, :, pl.ds(4 * tc, tc)] = b2
        mixed = part[0] + dot_nt(f2, mixall[l, :, pl.ds(2 * tc, tc)]) + dot_nt(b2, mixall[l, :, pl.ds(4 * tc, tc)])
        mixed = mixed + mbias[l:l + 1]
        hid = ext[l, :, pl.ds(0, tc)].astype(F32) + mixed
        if l + 1 < GATED_LAYERS:
            pack_s[0] = pack(hid)

            @pl.when(up)
            def _():
                shift_copy(1, pack_s.at[0], pack_r.at[0], 1).start()

            ext[l + 1, :, pl.ds(0, tc)] = hid.astype(BF)
        else:
            out[...] = hid.T.astype(BF)

    flow[...] = ctr[...]

    lane_g = lax.broadcasted_iota(jnp.int32, (ch, tc), 1) // ch

    def fold(x):
        y = x[0:ch]
        for t in range(1, steps):
            y = y + x[t * ch:(t + 1) * ch]
        sh = ch
        while sh < tc:
            y = y + pltpu.roll(y, sh, 1)
            sh *= 2
        return y

    def lanes_of(xs):
        y = jnp.zeros((ch, tc), F32)
        for g, x in enumerate(xs):
            y = jnp.where(lane_g == g, x, y)
        return y

    e_conv = None
    e_mix = [None, None]

    def gather_start(buf, ssem, rsem, count, here, copy):
        def go(off):
            p = lax.rem(here + off, count)
            copy(buf.at[here], buf.at[here], ssem.at[p], rsem.at[here], p).start()

        peers(count, go)

    def gather_sum(buf, ssem, rsem, count, here, copy):
        def take(off):
            p = lax.rem(here + off, count)
            copy(buf.at[p], buf.at[p], ssem.at[p], rsem.at[p], p).wait_recv()

        peers(count, take)
        total = buf[0]
        for p in range(1, count):
            total = total + buf[p]
        return total

    for l in reversed(range(GATED_LAYERS)):
        d = l + 1
        fr = flow[...].astype(BF)
        r0 = 2 * GATED_LAYERS + 2 * (GATED_LAYERS - 1 - l)

        def back(k):
            return dot(fr, mixall[l, :, pl.ds(k * tc, tc)])

        rest = []

        def fill_one():
            rest.extend([back(0), back(1), back(3)])
            prod = dot_tn(fr, hops[l])
            folds = [fold(jnp.where(same, prod[:, k * tc:(k + 1) * tc], 0.0)) for k in range(HOPS)]
            e_mix[l] = (lanes_of(folds[:4]), folds[4])
            if l == 0:
                e_buf[me] = jnp.concatenate(
                    [e_conv, e_mix[1][0], e_mix[0][0], lanes_of([e_mix[1][1], e_mix[0][1]])], axis=0
                )
                gather_start(e_buf, e_ssem, e_rsem, n_graph, me, graph_copy)

        bi, fi = pair(r0, back(4).astype(BF), back(2).astype(BF), fill_one)

        def fill_two():
            if l == 0:
                et_buf[z] = gather_sum(e_buf, e_ssem, e_rsem, n_graph, me, graph_copy)
                gather_start(et_buf, et_ssem, et_rsem, n_tm, z, tm_copy)

        bo, fo = pair(r0 + 1, (rest[2] + bi).astype(BF), (rest[1] + fi).astype(BF), fill_two)
        gg = rest[0] + fo + bo
        f = filt[l]
        g = gate[l]
        gf = gg * g * (1.0 - f * f)
        gt = gg * f * g * (1.0 - g)
        gp = jnp.concatenate([gf, gt], axis=1).astype(BF)
        slot = 2 + (GATED_LAYERS - 1 - l)
        at = 1 + (GATED_LAYERS - 1 - l)
        pack_s[at] = pack(dot(gp, band[l, :, pl.ds(tc, tc)]))

        @pl.when(down)
        def _():
            shift_copy(slot, pack_s.at[at], pack_r.at[at], -1).start()

        prod = dot_tn(gp, ext[l])
        pieces = []
        for tap in range(2):
            for h in range(2):
                own = prod[h * tc:(h + 1) * tc, :tc]
                if tap == 0:
                    x = jnp.where(same, own, 0.0)
                else:
                    x = jnp.where(before(d), own, 0.0) + jnp.where(before_prev(d), prod[h * tc:(h + 1) * tc, tc:], 0.0)
                pieces.append(fold(x))
        conv = lanes_of(pieces)
        if l == 0:
            l_buf[me] = conv
            gather_start(l_buf, l_ssem, l_rsem, n_graph, me, graph_copy)
        else:
            e_conv = conv
        new = flow[...] + dot(gp, band[l, :, pl.ds(0, tc)])

        @pl.when(up)
        def _():
            shift_copy(slot, pack_s.at[at], pack_r.at[at], -1).wait_recv()

        @pl.when(jnp.logical_not(up))
        def _():
            pack_r[at] = jnp.zeros((half_s, tc), BF)

        lanes = lax.broadcasted_iota(jnp.int32, (sensors, tc), 1)
        flow[...] = new + jnp.where(lanes >= tc // 2, unpack(pack_r[at]), 0.0)

    lt_buf[z] = gather_sum(l_buf, l_ssem, l_rsem, n_graph, me, graph_copy)
    gather_start(lt_buf, lt_ssem, lt_rsem, n_tm, z, tm_copy)
    gser[...] = flow[...].T.astype(BF)

    def lane_group(x, g):
        return (pltpu.roll(x, tc - g * ch, 1) if g else x)[:, :ch]

    def put_conv(l, x):
        for tap in range(2):
            for h in range(2):
                gconv[l, tap, pl.ds(h * ch, ch), :] = lane_group(x, tap * 2 + h)

    e = gather_sum(et_buf, et_ssem, et_rsem, n_tm, z, tm_copy) * scale
    put_conv(1, e[:ch])
    for k in range(4):
        gmix[1, k] = lane_group(e[ch:2 * ch], k)
        gmix[0, k] = lane_group(e[2 * ch:3 * ch], k)
    gmix[1, 4] = lane_group(e[3 * ch:], 0)
    gmix[0, 4] = lane_group(e[3 * ch:], 1)
    put_conv(0, gather_sum(lt_buf, lt_ssem, lt_rsem, n_tm, z, tm_copy) * scale)

    def sent_graph(off):
        p = lax.rem(me + off, n_graph)
        for r in range(4 * GATED_LAYERS):
            graph_copy(send.at[r, p], recv.at[r, me], r_ssem.at[r, p], r_rsem.at[r, me], p).wait_send()
        graph_copy(e_buf.at[me], e_buf.at[me], e_ssem.at[p], e_rsem.at[me], p).wait_send()
        graph_copy(l_buf.at[me], l_buf.at[me], l_ssem.at[p], l_rsem.at[me], p).wait_send()

    peers(n_graph, sent_graph)

    def sent_tm(off):
        p = lax.rem(z + off, n_tm)
        tm_copy(et_buf.at[z], et_buf.at[z], et_ssem.at[p], et_rsem.at[z], p).wait_send()
        tm_copy(lt_buf.at[z], lt_buf.at[z], lt_ssem.at[p], lt_rsem.at[z], p).wait_send()

    peers(n_tm, sent_tm)

    @pl.when(up)
    def _():
        first.wait_send()
        shift_copy(1, pack_s.at[0], pack_r.at[0], 1).wait_send()

    @pl.when(down)
    def _():
        shift_copy(2, pack_s.at[1], pack_r.at[1], -1).wait_send()
        shift_copy(3, pack_s.at[2], pack_r.at[2], -1).wait_send()


def per_device(series, cw, cb, mw, mb, tv, tcol, sidx, smask, cot):
    n_graph = lax.axis_size("graph")
    n_tm = lax.axis_size("tm")
    steps, ch, sensors = series.shape
    tc = steps * ch
    slots = sidx.shape[2]
    halo = n_graph * slots
    wire = BF if slots % 16 == 0 else F32
    rounds = 4 * GATED_LAYERS
    scale = 1.0 / math.sqrt(float(steps * n_tm * sensors * n_graph))
    vm = pl.BlockSpec(memory_space=pltpu.VMEM)
    sm = pl.BlockSpec(memory_space=pltpu.SMEM)
    dma = pltpu.SemaphoreType.DMA
    out, gser, gconv, gmix = pl.pallas_call(
        functools.partial(kernel, n_graph, n_tm, steps, scale),
        out_shape=(
            jax.ShapeDtypeStruct((tc, sensors), BF),
            jax.ShapeDtypeStruct((tc, sensors), BF),
            jax.ShapeDtypeStruct(cw.shape, F32),
            jax.ShapeDtypeStruct(mw.shape, F32),
        ),
        in_specs=[vm] * 6 + [sm] + [vm] * 3,
        out_specs=(vm,) * 4,
        scratch_shapes=[
            pltpu.VMEM((sensors, sensors), BF),
            pltpu.VMEM((sensors, sensors), BF),
            pltpu.VMEM((sensors, halo), BF),
            pltpu.VMEM((halo, sensors), BF),
            pltpu.VMEM((sensors, halo), BF),
            pltpu.VMEM((halo, sensors), BF),
            pltpu.VMEM((GATED_LAYERS, 2 * tc, 2 * tc), BF),
            pltpu.VMEM((GATED_LAYERS, tc, HOPS * tc), BF),
            pltpu.VMEM((GATED_LAYERS, sensors, 2 * tc), BF),
            pltpu.VMEM((GATED_LAYERS, sensors, HOPS * tc), BF),
            pltpu.VMEM((GATED_LAYERS, sensors, tc), F32),
            pltpu.VMEM((GATED_LAYERS, sensors, tc), F32),
            pltpu.VMEM((sensors, tc), F32),
            pltpu.VMEM((sensors, tc), F32),
            pltpu.VMEM((tc, sensors), BF),
            pltpu.VMEM((3, sensors // 2, tc), BF),
            pltpu.VMEM((3, sensors // 2, tc), BF),
            pltpu.VMEM((rounds, n_graph, 2, slots, tc), wire),
            pltpu.VMEM((rounds, n_graph, 2, slots, tc), wire),
            pltpu.VMEM((n_graph, 4 * ch, tc), F32),
            pltpu.VMEM((n_tm, 4 * ch, tc), F32),
            pltpu.VMEM((n_graph, ch, tc), F32),
            pltpu.VMEM((n_tm, ch, tc), F32),
            dma((rounds, n_graph)), dma((rounds, n_graph)),
            dma((4,)), dma((4,)),
            dma((n_graph,)), dma((n_graph,)),
            dma((n_tm,)), dma((n_tm,)),
            dma((n_graph,)), dma((n_graph,)),
            dma((n_tm,)), dma((n_tm,)),
        ],
        compiler_params=pltpu.CompilerParams(
            collective_id=0, has_side_effects=True, vmem_limit_bytes=48 * 1024 * 1024
        ),
    )(
        series.reshape(tc, sensors),
        cw.reshape(-1, ch),
        cb,
        mw.reshape(-1, ch),
        mb,
        tv.reshape(-1, *tv.shape[2:]),
        tcol,
        sidx[0],
        smask[0],
        cot.reshape(tc, sensors),
    )
    return out.reshape(series.shape), gser.reshape(series.shape), gconv, gmix


def solution(mesh):
    return jax.shard_map(
        per_device,
        mesh=mesh,
        in_specs=(
            P("tm", None, "graph"),
            P(),
            P(),
            P(),
            P(),
            P("graph", None, None, None),
            P("graph", None),
            P("graph", None, None),
            P("graph", None, None),
            P("tm", None, "graph"),
        ),
        out_specs=(P("tm", None, "graph"), P("tm", None, "graph"), P(), P()),
        check_vma=False,
    )
```

```python
import functools
import math

import jax
import jax.numpy as jnp
from jax import lax
from jax.experimental import pallas as pl
from jax.experimental.pallas import tpu as pltpu
from jax.sharding import PartitionSpec as P

GATED_LAYERS = 2
HOPS = 5
BF = jnp.bfloat16
F32 = jnp.float32
MESH = pl.DeviceIdType.MESH


def dot(a, b):
    return lax.dot_general(a, b, (((1,), (0,)), ((), ())), preferred_element_type=F32)


def dot_nt(a, b):
    return lax.dot_general(a, b, (((1,), (1,)), ((), ())), preferred_element_type=F32)


def dot_tn(a, b):
    return lax.dot_general(a, b, (((0,), (0,)), ((), ())), preferred_element_type=F32)


def peers(count, body):
    if count <= 8:
        for off in range(1, count):
            body(off)
    elif count > 1:
        lax.fori_loop(1, count, lambda off, c: (body(off), c)[1], 0)


def kernel(
    n_graph, n_tm, steps, scale,
    series_h, cw_h, cb_h, mw_h, mb_h, tv_h, tcol, sidx_h, smask_h, cot_h,
    out, gser, gconv, gmix,
    wl, wlt, wh, wht, gm, gmt, band, mixall, ext, hops, filt, gate, flow, ctr, hid_end,
    prev0, pack_s, pack_r, send, recv, e_buf, et_buf, l_buf, lt_buf,
    e_part, eg_buf, series, cw, cb, mw, mb, tv, sidx, smask, cot, in_sem,
    r_ssem, r_rsem, t_ssem, t_rsem, e_ssem, e_rsem, et_ssem, et_rsem,
    l_ssem, l_rsem, lt_ssem, lt_rsem, eg_ssem, eg_rsem,
):
    me = lax.axis_index("graph")
    z = lax.axis_index("tm")
    tc, sensors = series.shape
    ch = tc // steps
    half_s = sensors // 2
    slots = sidx.shape[1]
    halo = n_graph * slots
    tile = tv.shape[-1]
    rblocks, tslots = tcol.shape
    lblocks = sensors // tile
    hblocks = halo // tile
    wire = send.dtype
    er = e_part.shape[1]

    loads = [
        pltpu.make_async_copy(src, dst, in_sem.at[i])
        for i, (src, dst) in enumerate(
            ((cw_h, cw), (mw_h, mw), (cb_h, cb), (mb_h, mb), (tv_h, tv), (series_h, series),
             (sidx_h, sidx), (smask_h, smask), (cot_h, cot))
        )
    ]
    for load in loads:
        load.start()
    barrier = pltpu.get_barrier_semaphore()

    def greet_graph(off):
        pl.semaphore_signal(barrier, inc=1, device_id={"graph": lax.rem(me + off, n_graph)}, device_id_type=MESH)

    def greet_tm(off):
        pl.semaphore_signal(barrier, inc=1, device_id={"tm": lax.rem(z + off, n_tm)}, device_id_type=MESH)

    peers(n_graph, greet_graph)
    peers(n_tm, greet_tm)

    def shift_copy(slot, src, dst, by):
        return pltpu.make_async_remote_copy(
            src_ref=src, dst_ref=dst, send_sem=t_ssem.at[slot], recv_sem=t_rsem.at[slot],
            device_id={"tm": lax.rem(z + by + n_tm, n_tm)}, device_id_type=MESH,
        )

    up = z < n_tm - 1
    down = z > 0

    first = shift_copy(0, series_h.at[pl.ds(tc - ch, ch)], prev0.at[pl.ds(tc - ch, ch)], 1)
    prev0[pl.ds(0, tc - ch), :] = jnp.zeros((tc - ch, sensors), BF)

    row32 = lax.broadcasted_iota(jnp.int32, (ch, tc), 0)
    lane32 = lax.broadcasted_iota(jnp.int32, (ch, tc), 1)
    spread = jnp.where(lax.rem(lane32, ch) == row32, 1.0, 0.0)
    spread_b = spread.astype(BF)
    rt = lax.broadcasted_iota(jnp.int32, (tc, tc), 0) // ch
    lt = lax.broadcasted_iota(jnp.int32, (tc, tc), 1) // ch
    same = rt == lt

    def before(d):
        return lt == rt - d

    def before_prev(d):
        return lt == rt - d + steps

    for load in loads[:4]:
        load.wait()
    taps = 2 * GATED_LAYERS
    rs = lax.broadcasted_iota(jnp.int32, (taps * ch, taps * tc), 0)
    ls = lax.broadcasted_iota(jnp.int32, (taps * ch, taps * tc), 1)
    spread_taps = jnp.where((ls // tc) * ch + lax.rem(ls, ch) == rs, 1.0, 0.0).astype(BF)
    def after(d):
        return rt == lt - d

    def after_prev(d):
        return rt == lt - d + steps

    cwr = dot_tn(cw[...], spread_taps)
    mwr = dot(mw[...], spread_b)

    def stack(x, base):
        return jnp.concatenate([x[base:base + ch]] * steps, axis=0)

    for l in range(GATED_LAYERS):
        d = l + 1
        for h in range(2):
            w0 = stack(cwr[:, (l * 2) * tc:(l * 2 + 1) * tc], h * ch)
            w1 = stack(cwr[:, (l * 2 + 1) * tc:(l * 2 + 2) * tc], h * ch)
            own = jnp.where(same, w0, 0.0) + jnp.where(before(d), w1, 0.0)
            band[l, pl.ds(h * tc, tc), pl.ds(0, tc)] = own.astype(BF)
            band[l, pl.ds(h * tc, tc), pl.ds(tc, tc)] = jnp.where(before_prev(d), w1, 0.0).astype(BF)
        for k in range(HOPS):
            mk = stack(mwr, (l * HOPS + k) * ch)
            mixall[l, :, pl.ds(k * tc, tc)] = jnp.where(same, mk, 0.0).astype(BF)

    r64 = lax.broadcasted_iota(jnp.int32, (2 * ch, 2 * tc), 0)
    l64 = lax.broadcasted_iota(jnp.int32, (2 * ch, 2 * tc), 1)
    spread2 = jnp.where(lax.rem(l64, ch) + (l64 // tc) * ch == r64, 1.0, 0.0)
    cbias = lax.dot_general(cb[...], spread2, (((1,), (0,)), ((), ())), precision=lax.Precision.HIGHEST, preferred_element_type=F32)
    mbias = lax.dot_general(mb[...], spread, (((1,), (0,)), ((), ())), precision=lax.Precision.HIGHEST, preferred_element_type=F32)

    pl.semaphore_wait(barrier, n_graph - 1 + n_tm - 1)

    @pl.when(up)
    def _():
        first.start()

    for load in loads[4:]:
        load.wait()
    for r in range(rblocks):
        tiles = [tv[r * tslots + k].astype(F32) for k in range(tslots)]
        flips = [t.T for t in tiles]
        for c in range(lblocks + hblocks):
            a = jnp.zeros((tile, tile), F32)
            b = jnp.zeros((tile, tile), F32)
            for k in range(tslots):
                on = (tcol[r, k] == c).astype(jnp.int32).astype(F32)
                a = a + tiles[k] * on
                b = b + flips[k] * on
            a = a.astype(BF)
            b = b.astype(BF)
            if c < lblocks:
                wl[pl.ds(r * tile, tile), pl.ds(c * tile, tile)] = a
                wlt[pl.ds(c * tile, tile), pl.ds(r * tile, tile)] = b
            else:
                ch_at = c - lblocks
                wh[pl.ds(r * tile, tile), pl.ds(ch_at * tile, tile)] = a
                wht[pl.ds(ch_at * tile, tile), pl.ds(r * tile, tile)] = b

    key = jnp.where(smask[...] != 0, sidx[...] + 1, 0)
    es = lax.broadcasted_iota(jnp.int32, (slots, halo), 0)
    ej = lax.broadcasted_iota(jnp.int32, (slots, halo), 1)
    pick = jnp.where(lax.rem(ej, slots) == es, 1.0, 0.0).astype(BF)
    hi = dot((key // 32).astype(F32).astype(BF), pick)
    lo = dot(lax.rem(key, 32).astype(F32).astype(BF), pick)
    pr = lax.broadcasted_iota(jnp.int32, (n_graph, halo), 0)
    pj = lax.broadcasted_iota(jnp.int32, (n_graph, halo), 1) // slots
    keys = jnp.sum(jnp.where(pr == pj, hi * 32.0 + lo, 0.0), axis=0, keepdims=True)
    ids = lax.broadcasted_iota(jnp.int32, (sensors, halo), 0).astype(F32) + 1.0
    onehot = jnp.where(ids == keys, 1.0, 0.0)
    gm[...] = onehot.astype(BF)
    gmt[...] = onehot.T.astype(BF)

    ext[0, :, pl.ds(0, tc)] = series[...].astype(F32).T.astype(BF)

    def graph_copy(src, dst, ssem, rsem, p):
        return pltpu.make_async_remote_copy(
            src_ref=src, dst_ref=dst, send_sem=ssem, recv_sem=rsem,
            device_id={"graph": p}, device_id_type=MESH,
        )

    def tm_copy(src, dst, ssem, rsem, p):
        return pltpu.make_async_remote_copy(
            src_ref=src, dst_ref=dst, send_sem=ssem, recv_sem=rsem,
            device_id={"tm": p}, device_id_type=MESH,
        )

    def pair(r, pull_in, push_in, filler):
        sp = dot(gmt[...], pull_in)
        sb = dot(wht[...], push_in).astype(BF).astype(F32)
        send[r, :, 0] = sp.reshape(n_graph, slots, tc).astype(wire)
        send[r, :, 1] = sb.reshape(n_graph, slots, tc).astype(wire)

        def go(off):
            p = lax.rem(me + off, n_graph)
            graph_copy(send.at[r, p], recv.at[r, me], r_ssem.at[r, p], r_rsem.at[r, me], p).start()

        peers(n_graph, go)
        recv[r, me] = send[r, me]
        pulled = dot(wl[...], pull_in)
        pushed = dot(wlt[...], push_in)
        filler()

        def take(off):
            p = lax.rem(me + off, n_graph)
            graph_copy(send.at[r, p], recv.at[r, p], r_ssem.at[r, p], r_rsem.at[r, p], p).wait_recv()

        peers(n_graph, take)
        rp = recv[r, :, 0].astype(F32).reshape(halo, tc).astype(BF)
        rb = recv[r, :, 1].astype(F32).reshape(halo, tc).astype(BF)
        return pulled + dot(wh[...], rp), pushed + dot(gm[...], rb)

    lane_half = lax.broadcasted_iota(jnp.int32, (half_s, tc), 1) < tc // 2

    def pack(x):
        return jnp.where(lane_half, pltpu.roll(x[:half_s], tc // 2, 1), x[half_s:]).astype(BF)

    def unpack(p):
        x = p.astype(F32)
        return jnp.concatenate([pltpu.roll(x, tc // 2, 1), x], axis=0)

    def take_cotangent():
        ctr[...] = cot[...].astype(F32).T

    for l in range(GATED_LAYERS):
        if l == 0:
            @pl.when(down)
            def _():
                first.wait_recv()

            @pl.when(jnp.logical_not(down))
            def _():
                prev0[pl.ds(tc - ch, ch), :] = jnp.zeros((ch, sensors), BF)

            ext[0, :, pl.ds(tc, tc)] = prev0[...].astype(F32).T.astype(BF)
            pre = dot_nt(ext[0], band[0])
        else:
            pre_own = dot_nt(ext[l, :, pl.ds(0, tc)], band[l, :, pl.ds(0, tc)])

            @pl.when(down)
            def _():
                shift_copy(1, pack_s.at[0], pack_r.at[0], 1).wait_recv()

            @pl.when(jnp.logical_not(down))
            def _():
                pack_r[0] = jnp.zeros((half_s, tc), BF)

            ext[l, :, pl.ds(tc, tc)] = unpack(pack_r[0]).astype(BF)
            pre = pre_own + dot_nt(ext[l, :, pl.ds(tc, tc)], band[l, :, pl.ds(tc, tc)])
        pre = pre + cbias[l:l + 1]
        f = jnp.tanh(pre[:, :tc])
        g = jax.nn.sigmoid(pre[:, tc:])
        filt[l] = f
        gate[l] = g
        gated = (f * g).astype(BF)
        hops[l, :, pl.ds(0, tc)] = gated
        fo, bo = pair(2 * l, gated, gated, take_cotangent if l == 0 else (lambda: None))
        fo = fo.astype(BF)
        bo = bo.astype(BF)
        hops[l, :, pl.ds(tc, tc)] = fo
        hops[l, :, pl.ds(3 * tc, tc)] = bo
        part = []

        def mix_early():
            m = dot_nt(hops[l, :, pl.ds(0, 2 * tc)], mixall[l, :, pl.ds(0, 2 * tc)])
            part.append(m + dot_nt(hops[l, :, pl.ds(3 * tc, tc)], mixall[l, :, pl.ds(3 * tc, tc)]))

        f2, b2 = pair(2 * l + 1, fo, bo, mix_early)
        f2 = f2.astype(BF)
        b2 = b2.astype(BF)
        hops[l, :, pl.ds(2 * tc, tc)] = f2
        hops[l, :, pl.ds(4 * tc, tc)] = b2
        mixed = part[0] + dot_nt(f2, mixall[l, :, pl.ds(2 * tc, tc)]) + dot_nt(b2, mixall[l, :, pl.ds(4 * tc, tc)])
        mixed = mixed + mbias[l:l + 1]
        hid = ext[l, :, pl.ds(0, tc)].astype(F32) + mixed
        if l + 1 < GATED_LAYERS:
            pack_s[0] = pack(hid)

            @pl.when(up)
            def _():
                shift_copy(1, pack_s.at[0], pack_r.at[0], 1).start()

            ext[l + 1, :, pl.ds(0, tc)] = hid.astype(BF)
        else:
            hid_end[...] = hid

    flow[...] = ctr[...]

    lane_g = lax.broadcasted_iota(jnp.int32, (ch, tc), 1) // ch

    def fold(x):
        y = x[0:ch]
        for t in range(1, steps):
            y = y + x[t * ch:(t + 1) * ch]
        sh = ch
        while sh < tc:
            y = y + pltpu.roll(y, sh, 1)
            sh *= 2
        return y

    def lanes_of(xs):
        y = jnp.zeros((ch, tc), F32)
        for g, x in enumerate(xs):
            y = jnp.where(lane_g == g, x, y)
        return y

    e_conv = None
    e_mix = [None, None]

    def gather_start(buf, ssem, rsem, count, here, copy):
        def go(off):
            p = lax.rem(here + off, count)
            copy(buf.at[here], buf.at[here], ssem.at[p], rsem.at[here], p).start()

        peers(count, go)

    def gather_sum(buf, ssem, rsem, count, here, copy):
        def take(off):
            p = lax.rem(here + off, count)
            copy(buf.at[p], buf.at[p], ssem.at[p], rsem.at[p], p).wait_recv()

        peers(count, take)
        total = buf[0]
        for p in range(1, count):
            total = total + buf[p]
        return total

    for l in reversed(range(GATED_LAYERS)):
        d = l + 1
        fr = flow[...].astype(BF)
        r0 = 2 * GATED_LAYERS + 2 * (GATED_LAYERS - 1 - l)

        def back(k):
            return dot(fr, mixall[l, :, pl.ds(k * tc, tc)])

        rest = []

        def fill_one():
            rest.extend([back(0), back(1), back(3)])
            prod = dot_tn(fr, hops[l])
            folds = [fold(jnp.where(same, prod[:, k * tc:(k + 1) * tc], 0.0)) for k in range(HOPS)]
            if l == GATED_LAYERS - 1:
                out[...] = hid_end[...].T.astype(BF)
            e_mix[l] = (lanes_of(folds[:4]), folds[4])
            if l == 0:
                early = jnp.concatenate(
                    [e_conv, e_mix[1][0], e_mix[0][0], lanes_of([e_mix[1][1], e_mix[0][1]])], axis=0
                )
                for p in range(n_graph):
                    e_part[p] = early[p * er:(p + 1) * er]

                def scatter(off):
                    p = lax.rem(me + off, n_graph)
                    graph_copy(e_part.at[p], e_buf.at[me], e_ssem.at[p], e_rsem.at[me], p).start()

                peers(n_graph, scatter)
                e_buf[me] = e_part[me]

        bi, fi = pair(r0, back(4).astype(BF), back(2).astype(BF), fill_one)

        def fill_two():
            if l == 0:
                et_buf[z] = gather_sum(e_buf, e_ssem, e_rsem, n_graph, me, graph_copy)
                gather_start(et_buf, et_ssem, et_rsem, n_tm, z, tm_copy)

        bo, fo = pair(r0 + 1, (rest[2] + bi).astype(BF), (rest[1] + fi).astype(BF), fill_two)
        gg = rest[0] + fo + bo
        f = filt[l]
        g = gate[l]
        gf = gg * g * (1.0 - f * f)
        gt = gg * f * g * (1.0 - g)
        gp = jnp.concatenate([gf, gt], axis=1).astype(BF)
        slot = 2 + (GATED_LAYERS - 1 - l)
        at = 1 + (GATED_LAYERS - 1 - l)
        pack_s[at] = pack(dot(gp, band[l, :, pl.ds(tc, tc)]))

        @pl.when(down)
        def _():
            shift_copy(slot, pack_s.at[at], pack_r.at[at], -1).start()

        prod = dot_tn(ext[l], gp)
        pieces = []
        for tap in range(2):
            for h in range(2):
                own = prod[:tc, h * tc:(h + 1) * tc]
                if tap == 0:
                    x = jnp.where(same, own, 0.0)
                else:
                    x = jnp.where(after(d), own, 0.0) + jnp.where(after_prev(d), prod[tc:, h * tc:(h + 1) * tc], 0.0)
                pieces.append(fold(x))
        conv = lanes_of(pieces)
        if l == 0:
            l_buf[me] = conv
            gather_start(l_buf, l_ssem, l_rsem, n_graph, me, graph_copy)
            eg_buf[me] = gather_sum(et_buf, et_ssem, et_rsem, n_tm, z, tm_copy)
            gather_start(eg_buf, eg_ssem, eg_rsem, n_graph, me, graph_copy)
        else:
            e_conv = conv
        new = flow[...] + dot(gp, band[l, :, pl.ds(0, tc)])

        @pl.when(up)
        def _():
            shift_copy(slot, pack_s.at[at], pack_r.at[at], -1).wait_recv()

        @pl.when(jnp.logical_not(up))
        def _():
            pack_r[at] = jnp.zeros((half_s, tc), BF)

        lanes = lax.broadcasted_iota(jnp.int32, (sensors, tc), 1)
        flow[...] = new + jnp.where(lanes >= tc // 2, unpack(pack_r[at]), 0.0)

    lt_buf[z] = gather_sum(l_buf, l_ssem, l_rsem, n_graph, me, graph_copy)
    gather_start(lt_buf, lt_ssem, lt_rsem, n_tm, z, tm_copy)
    gser[...] = flow[...].T.astype(BF)

    def lane_group(x, g):
        return (pltpu.roll(x, tc - g * ch, 1) if g else x)[:, :ch]

    def put_conv(l, x):
        gconv[l, 0] = x[:, :2 * ch]
        gconv[l, 1] = pltpu.roll(x, tc - 2 * ch, 1)[:, :2 * ch]

    def take_group(off):
        p = lax.rem(me + off, n_graph)
        graph_copy(eg_buf.at[p], eg_buf.at[p], eg_ssem.at[p], eg_rsem.at[p], p).wait_recv()

    peers(n_graph, take_group)
    e = jnp.concatenate([eg_buf[p] for p in range(n_graph)], axis=0) * scale
    put_conv(1, e[:ch])
    for k in range(4):
        gmix[1, k] = lane_group(e[ch:2 * ch], k)
        gmix[0, k] = lane_group(e[2 * ch:3 * ch], k)
    gmix[1, 4] = lane_group(e[3 * ch:], 0)
    gmix[0, 4] = lane_group(e[3 * ch:], 1)
    put_conv(0, gather_sum(lt_buf, lt_ssem, lt_rsem, n_tm, z, tm_copy) * scale)

    def sent_graph(off):
        p = lax.rem(me + off, n_graph)
        for r in range(4 * GATED_LAYERS):
            graph_copy(send.at[r, p], recv.at[r, me], r_ssem.at[r, p], r_rsem.at[r, me], p).wait_send()
        graph_copy(e_part.at[p], e_buf.at[me], e_ssem.at[p], e_rsem.at[me], p).wait_send()
        graph_copy(eg_buf.at[me], eg_buf.at[me], eg_ssem.at[p], eg_rsem.at[me], p).wait_send()
        graph_copy(l_buf.at[me], l_buf.at[me], l_ssem.at[p], l_rsem.at[me], p).wait_send()

    peers(n_graph, sent_graph)

    def sent_tm(off):
        p = lax.rem(z + off, n_tm)
        tm_copy(et_buf.at[z], et_buf.at[z], et_ssem.at[p], et_rsem.at[z], p).wait_send()
        tm_copy(lt_buf.at[z], lt_buf.at[z], lt_ssem.at[p], lt_rsem.at[z], p).wait_send()

    peers(n_tm, sent_tm)

    @pl.when(up)
    def _():
        first.wait_send()
        shift_copy(1, pack_s.at[0], pack_r.at[0], 1).wait_send()

    @pl.when(down)
    def _():
        shift_copy(2, pack_s.at[1], pack_r.at[1], -1).wait_send()
        shift_copy(3, pack_s.at[2], pack_r.at[2], -1).wait_send()


def store_kernel(a, b, c, d, ao, bo, co, do, sem):
    copies = [
        pltpu.make_async_copy(src, dst, sem.at[i])
        for i, (src, dst) in enumerate(((a, ao), (b, bo), (c, co), (d, do)))
    ]
    for copy in copies:
        copy.start()
    for copy in copies:
        copy.wait()


def per_device(series, cw, cb, mw, mb, tv, tcol, sidx, smask, cot):
    n_graph = lax.axis_size("graph")
    n_tm = lax.axis_size("tm")
    steps, ch, sensors = series.shape
    tc = steps * ch
    slots = sidx.shape[2]
    halo = n_graph * slots
    wire = BF if slots % 16 == 0 else F32
    rounds = 4 * GATED_LAYERS
    scale = 1.0 / math.sqrt(float(steps * n_tm * sensors * n_graph))
    vm = pl.BlockSpec(memory_space=pltpu.VMEM)
    hb = pl.BlockSpec(memory_space=pltpu.HBM)
    cwt_shape = (*cw.shape[:2], cw.shape[3], cw.shape[2])
    ins = (
        series.reshape(tc, sensors),
        jnp.swapaxes(cw, 2, 3).reshape(-1, cw.shape[2]),
        cb,
        mw.reshape(-1, ch),
        mb,
        tv.reshape(-1, *tv.shape[2:]),
        tcol,
        sidx[0],
        smask[0],
        cot.reshape(tc, sensors),
    )
    er = 4 * ch // n_graph
    sm = pl.BlockSpec(memory_space=pltpu.SMEM)
    dma = pltpu.SemaphoreType.DMA
    out, gser, gconv, gmix = pl.pallas_call(
        functools.partial(kernel, n_graph, n_tm, steps, scale),
        out_shape=(
            jax.ShapeDtypeStruct((tc, sensors), BF),
            jax.ShapeDtypeStruct((tc, sensors), BF),
            jax.ShapeDtypeStruct(cwt_shape, F32),
            jax.ShapeDtypeStruct(mw.shape, F32),
        ),
        in_specs=[hb] * 6 + [sm] + [hb] * 3,
        out_specs=(vm,) * 4,
        scratch_shapes=[
            pltpu.VMEM((sensors, sensors), BF),
            pltpu.VMEM((sensors, sensors), BF),
            pltpu.VMEM((sensors, halo), BF),
            pltpu.VMEM((halo, sensors), BF),
            pltpu.VMEM((sensors, halo), BF),
            pltpu.VMEM((halo, sensors), BF),
            pltpu.VMEM((GATED_LAYERS, 2 * tc, 2 * tc), BF),
            pltpu.VMEM((GATED_LAYERS, tc, HOPS * tc), BF),
            pltpu.VMEM((GATED_LAYERS, sensors, 2 * tc), BF),
            pltpu.VMEM((GATED_LAYERS, sensors, HOPS * tc), BF),
            pltpu.VMEM((GATED_LAYERS, sensors, tc), F32),
            pltpu.VMEM((GATED_LAYERS, sensors, tc), F32),
            pltpu.VMEM((sensors, tc), F32),
            pltpu.VMEM((sensors, tc), F32),
            pltpu.VMEM((sensors, tc), F32),
            pltpu.VMEM((tc, sensors), BF),
            pltpu.VMEM((3, sensors // 2, tc), BF),
            pltpu.VMEM((3, sensors // 2, tc), BF),
            pltpu.VMEM((rounds, n_graph, 2, slots, tc), wire),
            pltpu.VMEM((rounds, n_graph, 2, slots, tc), wire),
            pltpu.VMEM((n_graph, er, tc), F32),
            pltpu.VMEM((n_tm, er, tc), F32),
            pltpu.VMEM((n_graph, ch, tc), F32),
            pltpu.VMEM((n_tm, ch, tc), F32),
            pltpu.VMEM((n_graph, er, tc), F32),
            pltpu.VMEM((n_graph, er, tc), F32),
            *[pltpu.VMEM(x.shape, x.dtype) for x in ins[:6] + ins[7:]],
            dma((9,)),
            dma((rounds, n_graph)), dma((rounds, n_graph)),
            dma((4,)), dma((4,)),
            dma((n_graph,)), dma((n_graph,)),
            dma((n_tm,)), dma((n_tm,)),
            dma((n_graph,)), dma((n_graph,)),
            dma((n_tm,)), dma((n_tm,)),
            dma((n_graph,)), dma((n_graph,)),
        ],
        compiler_params=pltpu.CompilerParams(
            collective_id=0, has_side_effects=True, vmem_limit_bytes=63 * 1024 * 1024
        ),
    )(*ins)
    results = (out, gser, gconv, gmix)
    out, gser, gconv, gmix = pl.pallas_call(
        store_kernel,
        out_shape=tuple(jax.ShapeDtypeStruct(x.shape, x.dtype) for x in results),
        in_specs=[hb] * 4,
        out_specs=(hb,) * 4,
        scratch_shapes=[dma((4,))],
    )(*results)
    gconv = jnp.swapaxes(gconv, 2, 3)
    return out.reshape(series.shape), gser.reshape(series.shape), gconv, gmix


def solution(mesh):
    return jax.shard_map(
        per_device,
        mesh=mesh,
        in_specs=(
            P("tm", None, "graph"),
            P(),
            P(),
            P(),
            P(),
            P("graph", None, None, None),
            P("graph", None),
            P("graph", None, None),
            P("graph", None, None),
            P("tm", None, "graph"),
        ),
        out_specs=(P("tm", None, "graph"), P("tm", None, "graph"), P(), P()),
        check_vma=False,
    )
```

```python
import functools
import math

import jax
import jax.numpy as jnp
from jax import lax
from jax.experimental import pallas as pl
from jax.experimental.pallas import tpu as pltpu
from jax.sharding import PartitionSpec as P

GATED_LAYERS = 2
HOPS = 5
BF = jnp.bfloat16
F32 = jnp.float32
MESH = pl.DeviceIdType.MESH


def dot(a, b):
    return lax.dot_general(a, b, (((1,), (0,)), ((), ())), preferred_element_type=F32)


def dot_nt(a, b):
    return lax.dot_general(a, b, (((1,), (1,)), ((), ())), preferred_element_type=F32)


def dot_tn(a, b):
    return lax.dot_general(a, b, (((0,), (0,)), ((), ())), preferred_element_type=F32)


def peers(count, body):
    if count <= 8:
        for off in range(count - 1, 0, -1):
            body(off)
    elif count > 1:
        lax.fori_loop(1, count, lambda off, c: (body(off), c)[1], 0)


def kernel(
    n_graph, n_tm, steps, scale,
    series_h, cw_h, cb_h, mw_h, mb_h, tv_h, tcol, sidx_h, smask_h, cot_h,
    out, gser, gconv, gmix,
    wl, wlt, wh, wht, gm, gmt, band, mixall, ext, hops, filt, gate, flow, ctr, hid_end,
    prev0, pack_s, pack_r, send, recv, e_buf, et_buf, l_buf, lt_buf,
    e_part, eg_buf, series, cw, cb, mw, mb, tv, sidx, smask, cot, in_sem,
    r_ssem, r_rsem, t_ssem, t_rsem, e_ssem, e_rsem, et_ssem, et_rsem,
    l_ssem, l_rsem, lt_ssem, lt_rsem, eg_ssem, eg_rsem,
):
    me = lax.axis_index("graph")
    z = lax.axis_index("tm")
    tc, sensors = series.shape
    ch = tc // steps
    half_s = sensors // 2
    slots = sidx.shape[1]
    halo = n_graph * slots
    tile = tv.shape[-1]
    rblocks, tslots = tcol.shape
    lblocks = sensors // tile
    hblocks = halo // tile
    wire = send.dtype

    def partner(off):
        if n_graph & (n_graph - 1) or n_graph > 8:
            return lax.rem(me + off, n_graph)
        p = 0
        bit = 1
        while bit < n_graph:
            p = p + lax.rem(me // bit + off // bit, 2) * bit
            bit *= 2
        return p

    er = e_part.shape[1]

    loads = [
        pltpu.make_async_copy(src, dst, in_sem.at[i])
        for i, (src, dst) in enumerate(
            ((cw_h, cw), (mw_h, mw), (cb_h, cb), (mb_h, mb), (tv_h, tv), (series_h, series),
             (sidx_h, sidx), (smask_h, smask), (cot_h, cot))
        )
    ]
    for load in loads:
        load.start()
    barrier = pltpu.get_barrier_semaphore()

    def greet_graph(off):
        pl.semaphore_signal(barrier, inc=1, device_id={"graph": partner(off)}, device_id_type=MESH)

    def greet_tm(off):
        pl.semaphore_signal(barrier, inc=1, device_id={"tm": lax.rem(z + off, n_tm)}, device_id_type=MESH)

    peers(n_graph, greet_graph)
    peers(n_tm, greet_tm)

    def shift_copy(slot, src, dst, by):
        return pltpu.make_async_remote_copy(
            src_ref=src, dst_ref=dst, send_sem=t_ssem.at[slot], recv_sem=t_rsem.at[slot],
            device_id={"tm": lax.rem(z + by + n_tm, n_tm)}, device_id_type=MESH,
        )

    up = z < n_tm - 1
    down = z > 0

    first = shift_copy(0, series_h.at[pl.ds(tc - ch, ch)], prev0.at[pl.ds(tc - ch, ch)], 1)
    prev0[pl.ds(0, tc - ch), :] = jnp.zeros((tc - ch, sensors), BF)

    row32 = lax.broadcasted_iota(jnp.int32, (ch, tc), 0)
    lane32 = lax.broadcasted_iota(jnp.int32, (ch, tc), 1)
    spread = jnp.where(lax.rem(lane32, ch) == row32, 1.0, 0.0)
    spread_b = spread.astype(BF)
    rt = lax.broadcasted_iota(jnp.int32, (tc, tc), 0) // ch
    lt = lax.broadcasted_iota(jnp.int32, (tc, tc), 1) // ch
    same = rt == lt

    def before(d):
        return lt == rt - d

    def before_prev(d):
        return lt == rt - d + steps

    for load in loads[:4]:
        load.wait()
    taps = 2 * GATED_LAYERS
    rs = lax.broadcasted_iota(jnp.int32, (taps * ch, taps * tc), 0)
    ls = lax.broadcasted_iota(jnp.int32, (taps * ch, taps * tc), 1)
    spread_taps = jnp.where((ls // tc) * ch + lax.rem(ls, ch) == rs, 1.0, 0.0).astype(BF)
    def after(d):
        return rt == lt - d

    def after_prev(d):
        return rt == lt - d + steps

    cwr = dot_tn(cw[...], spread_taps)
    mwr = dot(mw[...], spread_b)

    def stack(x, base):
        return jnp.concatenate([x[base:base + ch]] * steps, axis=0)

    for l in range(GATED_LAYERS):
        d = l + 1
        for h in range(2):
            w0 = stack(cwr[:, (l * 2) * tc:(l * 2 + 1) * tc], h * ch)
            w1 = stack(cwr[:, (l * 2 + 1) * tc:(l * 2 + 2) * tc], h * ch)
            own = jnp.where(same, w0, 0.0) + jnp.where(before(d), w1, 0.0)
            band[l, pl.ds(h * tc, tc), pl.ds(0, tc)] = own.astype(BF)
            band[l, pl.ds(h * tc, tc), pl.ds(tc, tc)] = jnp.where(before_prev(d), w1, 0.0).astype(BF)
        for k in range(HOPS):
            mk = stack(mwr, (l * HOPS + k) * ch)
            mixall[l, :, pl.ds(k * tc, tc)] = jnp.where(same, mk, 0.0).astype(BF)

    r64 = lax.broadcasted_iota(jnp.int32, (2 * ch, 2 * tc), 0)
    l64 = lax.broadcasted_iota(jnp.int32, (2 * ch, 2 * tc), 1)
    spread2 = jnp.where(lax.rem(l64, ch) + (l64 // tc) * ch == r64, 1.0, 0.0)
    cbias = lax.dot_general(cb[...], spread2, (((1,), (0,)), ((), ())), precision=lax.Precision.HIGHEST, preferred_element_type=F32)
    mbias = lax.dot_general(mb[...], spread, (((1,), (0,)), ((), ())), precision=lax.Precision.HIGHEST, preferred_element_type=F32)

    pl.semaphore_wait(barrier, n_graph - 1 + n_tm - 1)

    @pl.when(up)
    def _():
        first.start()

    for load in loads[4:]:
        load.wait()
    for r in range(rblocks):
        tiles = [tv[r * tslots + k].astype(F32) for k in range(tslots)]
        flips = [t.T for t in tiles]
        for c in range(lblocks + hblocks):
            a = jnp.zeros((tile, tile), F32)
            b = jnp.zeros((tile, tile), F32)
            for k in range(tslots):
                on = (tcol[r, k] == c).astype(jnp.int32).astype(F32)
                a = a + tiles[k] * on
                b = b + flips[k] * on
            a = a.astype(BF)
            b = b.astype(BF)
            if c < lblocks:
                wl[pl.ds(r * tile, tile), pl.ds(c * tile, tile)] = a
                wlt[pl.ds(c * tile, tile), pl.ds(r * tile, tile)] = b
            else:
                ch_at = c - lblocks
                wh[pl.ds(r * tile, tile), pl.ds(ch_at * tile, tile)] = a
                wht[pl.ds(ch_at * tile, tile), pl.ds(r * tile, tile)] = b

    key = jnp.where(smask[...] != 0, sidx[...] + 1, 0)
    es = lax.broadcasted_iota(jnp.int32, (slots, halo), 0)
    ej = lax.broadcasted_iota(jnp.int32, (slots, halo), 1)
    pick = jnp.where(lax.rem(ej, slots) == es, 1.0, 0.0).astype(BF)
    hi = dot((key // 32).astype(F32).astype(BF), pick)
    lo = dot(lax.rem(key, 32).astype(F32).astype(BF), pick)
    pr = lax.broadcasted_iota(jnp.int32, (n_graph, halo), 0)
    pj = lax.broadcasted_iota(jnp.int32, (n_graph, halo), 1) // slots
    keys = jnp.sum(jnp.where(pr == pj, hi * 32.0 + lo, 0.0), axis=0, keepdims=True)
    ids = lax.broadcasted_iota(jnp.int32, (sensors, halo), 0).astype(F32) + 1.0
    onehot = jnp.where(ids == keys, 1.0, 0.0)
    gm[...] = onehot.astype(BF)
    gmt[...] = onehot.T.astype(BF)

    ext[0, :, pl.ds(0, tc)] = series[...].astype(F32).T.astype(BF)

    def graph_copy(src, dst, ssem, rsem, p):
        return pltpu.make_async_remote_copy(
            src_ref=src, dst_ref=dst, send_sem=ssem, recv_sem=rsem,
            device_id={"graph": p}, device_id_type=MESH,
        )

    def tm_copy(src, dst, ssem, rsem, p):
        return pltpu.make_async_remote_copy(
            src_ref=src, dst_ref=dst, send_sem=ssem, recv_sem=rsem,
            device_id={"tm": p}, device_id_type=MESH,
        )

    def pair(r, pull_in, push_in, filler):
        sp = dot(gmt[...], pull_in)
        sb = dot(wht[...], push_in).astype(BF).astype(F32)
        send[r, :, 0] = sp.reshape(n_graph, slots, tc).astype(wire)
        send[r, :, 1] = sb.reshape(n_graph, slots, tc).astype(wire)

        def go(off):
            p = partner(off)
            graph_copy(send.at[r, p], recv.at[r, me], r_ssem.at[r, p], r_rsem.at[r, me], p).start()

        peers(n_graph, go)
        recv[r, me] = send[r, me]
        pulled = dot(wl[...], pull_in)
        pushed = dot(wlt[...], push_in)
        filler()

        def take(off):
            p = partner(off)
            graph_copy(send.at[r, p], recv.at[r, p], r_ssem.at[r, p], r_rsem.at[r, p], p).wait_recv()

        peers(n_graph, take)
        rp = recv[r, :, 0].astype(F32).reshape(halo, tc).astype(BF)
        rb = recv[r, :, 1].astype(F32).reshape(halo, tc).astype(BF)
        return pulled + dot(wh[...], rp), pushed + dot(gm[...], rb)

    lane_half = lax.broadcasted_iota(jnp.int32, (half_s, tc), 1) < tc // 2

    def pack(x):
        return jnp.where(lane_half, pltpu.roll(x[:half_s], tc // 2, 1), x[half_s:]).astype(BF)

    def unpack(p):
        x = p.astype(F32)
        return jnp.concatenate([pltpu.roll(x, tc // 2, 1), x], axis=0)

    def take_cotangent():
        ctr[...] = cot[...].astype(F32).T

    for l in range(GATED_LAYERS):
        if l == 0:
            @pl.when(down)
            def _():
                first.wait_recv()

            @pl.when(jnp.logical_not(down))
            def _():
                prev0[pl.ds(tc - ch, ch), :] = jnp.zeros((ch, sensors), BF)

            ext[0, :, pl.ds(tc, tc)] = prev0[...].astype(F32).T.astype(BF)
            pre = dot_nt(ext[0], band[0])
        else:
            pre_own = dot_nt(ext[l, :, pl.ds(0, tc)], band[l, :, pl.ds(0, tc)])

            @pl.when(down)
            def _():
                shift_copy(1, pack_s.at[0], pack_r.at[0], 1).wait_recv()

            @pl.when(jnp.logical_not(down))
            def _():
                pack_r[0] = jnp.zeros((half_s, tc), BF)

            ext[l, :, pl.ds(tc, tc)] = unpack(pack_r[0]).astype(BF)
            pre = pre_own + dot_nt(ext[l, :, pl.ds(tc, tc)], band[l, :, pl.ds(tc, tc)])
        pre = pre + cbias[l:l + 1]
        f = jnp.tanh(pre[:, :tc])
        g = jax.nn.sigmoid(pre[:, tc:])
        filt[l] = f
        gate[l] = g
        gated = (f * g).astype(BF)
        hops[l, :, pl.ds(0, tc)] = gated
        fo, bo = pair(2 * l, gated, gated, take_cotangent if l == 0 else (lambda: None))
        fo = fo.astype(BF)
        bo = bo.astype(BF)
        hops[l, :, pl.ds(tc, tc)] = fo
        hops[l, :, pl.ds(3 * tc, tc)] = bo
        part = []

        def mix_early():
            m = dot_nt(hops[l, :, pl.ds(0, 2 * tc)], mixall[l, :, pl.ds(0, 2 * tc)])
            part.append(m + dot_nt(hops[l, :, pl.ds(3 * tc, tc)], mixall[l, :, pl.ds(3 * tc, tc)]))

        f2, b2 = pair(2 * l + 1, fo, bo, mix_early)
        f2 = f2.astype(BF)
        b2 = b2.astype(BF)
        hops[l, :, pl.ds(2 * tc, tc)] = f2
        hops[l, :, pl.ds(4 * tc, tc)] = b2
        mixed = part[0] + dot_nt(f2, mixall[l, :, pl.ds(2 * tc, tc)]) + dot_nt(b2, mixall[l, :, pl.ds(4 * tc, tc)])
        mixed = mixed + mbias[l:l + 1]
        hid = ext[l, :, pl.ds(0, tc)].astype(F32) + mixed
        if l + 1 < GATED_LAYERS:
            pack_s[0] = pack(hid)

            @pl.when(up)
            def _():
                shift_copy(1, pack_s.at[0], pack_r.at[0], 1).start()

            ext[l + 1, :, pl.ds(0, tc)] = hid.astype(BF)
        else:
            hid_end[...] = hid

    flow[...] = ctr[...]

    lane_g = lax.broadcasted_iota(jnp.int32, (ch, tc), 1) // ch

    def fold(x):
        y = x[0:ch]
        for t in range(1, steps):
            y = y + x[t * ch:(t + 1) * ch]
        sh = ch
        while sh < tc:
            y = y + pltpu.roll(y, sh, 1)
            sh *= 2
        return y

    def lanes_of(xs):
        y = jnp.zeros((ch, tc), F32)
        for g, x in enumerate(xs):
            y = jnp.where(lane_g == g, x, y)
        return y

    e_conv = None
    e_mix = [None, None]

    def gather_start(buf, ssem, rsem, count, here, copy):
        def go(off):
            p = lax.rem(here + off, count)
            copy(buf.at[here], buf.at[here], ssem.at[p], rsem.at[here], p).start()

        peers(count, go)

    def gather_sum(buf, ssem, rsem, count, here, copy):
        def take(off):
            p = lax.rem(here + off, count)
            copy(buf.at[p], buf.at[p], ssem.at[p], rsem.at[p], p).wait_recv()

        peers(count, take)
        total = buf[0]
        for p in range(1, count):
            total = total + buf[p]
        return total

    for l in reversed(range(GATED_LAYERS)):
        d = l + 1
        fr = flow[...].astype(BF)
        r0 = 2 * GATED_LAYERS + 2 * (GATED_LAYERS - 1 - l)

        def back(k):
            return dot(fr, mixall[l, :, pl.ds(k * tc, tc)])

        rest = []

        def fill_one():
            rest.extend([back(0), back(1), back(3)])
            prod = dot_tn(fr, hops[l])
            folds = [fold(jnp.where(same, prod[:, k * tc:(k + 1) * tc], 0.0)) for k in range(HOPS)]
            if l == GATED_LAYERS - 1:
                out[...] = hid_end[...].T.astype(BF)
            e_mix[l] = (lanes_of(folds[:4]), folds[4])
            if l == 0:
                early = jnp.concatenate(
                    [e_conv, e_mix[1][0], e_mix[0][0], lanes_of([e_mix[1][1], e_mix[0][1]])], axis=0
                )
                for p in range(n_graph):
                    e_part[p] = early[p * er:(p + 1) * er]

                def scatter(off):
                    p = partner(off)
                    graph_copy(e_part.at[p], e_buf.at[me], e_ssem.at[p], e_rsem.at[me], p).start()

                peers(n_graph, scatter)
                e_buf[me] = e_part[me]

        bi, fi = pair(r0, back(4).astype(BF), back(2).astype(BF), fill_one)

        def fill_two():
            if l == 0:
                et_buf[z] = gather_sum(e_buf, e_ssem, e_rsem, n_graph, me, graph_copy)
                gather_start(et_buf, et_ssem, et_rsem, n_tm, z, tm_copy)

        bo, fo = pair(r0 + 1, (rest[2] + bi).astype(BF), (rest[1] + fi).astype(BF), fill_two)
        gg = rest[0] + fo + bo
        f = filt[l]
        g = gate[l]
        gf = gg * g * (1.0 - f * f)
        gt = gg * f * g * (1.0 - g)
        gp = jnp.concatenate([gf, gt], axis=1).astype(BF)
        slot = 2 + (GATED_LAYERS - 1 - l)
        at = 1 + (GATED_LAYERS - 1 - l)
        pack_s[at] = pack(dot(gp, band[l, :, pl.ds(tc, tc)]))

        @pl.when(down)
        def _():
            shift_copy(slot, pack_s.at[at], pack_r.at[at], -1).start()

        prod = dot_tn(ext[l], gp)
        pieces = []
        for tap in range(2):
            for h in range(2):
                own = prod[:tc, h * tc:(h + 1) * tc]
                if tap == 0:
                    x = jnp.where(same, own, 0.0)
                else:
                    x = jnp.where(after(d), own, 0.0) + jnp.where(after_prev(d), prod[tc:, h * tc:(h + 1) * tc], 0.0)
                pieces.append(fold(x))
        conv = lanes_of(pieces)
        if l == 0:
            l_buf[me] = conv
            gather_start(l_buf, l_ssem, l_rsem, n_graph, me, graph_copy)
            eg_buf[me] = gather_sum(et_buf, et_ssem, et_rsem, n_tm, z, tm_copy)
            gather_start(eg_buf, eg_ssem, eg_rsem, n_graph, me, graph_copy)
        else:
            e_conv = conv
        new = flow[...] + dot(gp, band[l, :, pl.ds(0, tc)])

        @pl.when(up)
        def _():
            shift_copy(slot, pack_s.at[at], pack_r.at[at], -1).wait_recv()

        @pl.when(jnp.logical_not(up))
        def _():
            pack_r[at] = jnp.zeros((half_s, tc), BF)

        lanes = lax.broadcasted_iota(jnp.int32, (sensors, tc), 1)
        flow[...] = new + jnp.where(lanes >= tc // 2, unpack(pack_r[at]), 0.0)

    lt_buf[z] = gather_sum(l_buf, l_ssem, l_rsem, n_graph, me, graph_copy)
    gather_start(lt_buf, lt_ssem, lt_rsem, n_tm, z, tm_copy)
    gser[...] = flow[...].T.astype(BF)

    def lane_group(x, g):
        return (pltpu.roll(x, tc - g * ch, 1) if g else x)[:, :ch]

    def put_conv(l, x):
        gconv[l, 0] = x[:, :2 * ch]
        gconv[l, 1] = pltpu.roll(x, tc - 2 * ch, 1)[:, :2 * ch]

    def take_group(off):
        p = partner(off)
        graph_copy(eg_buf.at[p], eg_buf.at[p], eg_ssem.at[p], eg_rsem.at[p], p).wait_recv()

    peers(n_graph, take_group)
    e = jnp.concatenate([eg_buf[p] for p in range(n_graph)], axis=0) * scale
    put_conv(1, e[:ch])
    for k in range(4):
        gmix[1, k] = lane_group(e[ch:2 * ch], k)
        gmix[0, k] = lane_group(e[2 * ch:3 * ch], k)
    gmix[1, 4] = lane_group(e[3 * ch:], 0)
    gmix[0, 4] = lane_group(e[3 * ch:], 1)
    put_conv(0, gather_sum(lt_buf, lt_ssem, lt_rsem, n_tm, z, tm_copy) * scale)

    def sent_graph(off):
        p = partner(off)
        for r in range(4 * GATED_LAYERS):
            graph_copy(send.at[r, p], recv.at[r, me], r_ssem.at[r, p], r_rsem.at[r, me], p).wait_send()
        graph_copy(e_part.at[p], e_buf.at[me], e_ssem.at[p], e_rsem.at[me], p).wait_send()
        graph_copy(eg_buf.at[me], eg_buf.at[me], eg_ssem.at[p], eg_rsem.at[me], p).wait_send()
        graph_copy(l_buf.at[me], l_buf.at[me], l_ssem.at[p], l_rsem.at[me], p).wait_send()

    peers(n_graph, sent_graph)

    def sent_tm(off):
        p = lax.rem(z + off, n_tm)
        tm_copy(et_buf.at[z], et_buf.at[z], et_ssem.at[p], et_rsem.at[z], p).wait_send()
        tm_copy(lt_buf.at[z], lt_buf.at[z], lt_ssem.at[p], lt_rsem.at[z], p).wait_send()

    peers(n_tm, sent_tm)

    @pl.when(up)
    def _():
        first.wait_send()
        shift_copy(1, pack_s.at[0], pack_r.at[0], 1).wait_send()

    @pl.when(down)
    def _():
        shift_copy(2, pack_s.at[1], pack_r.at[1], -1).wait_send()
        shift_copy(3, pack_s.at[2], pack_r.at[2], -1).wait_send()


def store_kernel(a, b, c, d, ao, bo, co, do):
    ao[...] = a[...]
    bo[...] = b[...]
    co[...] = c[...]
    do[...] = d[...]


def per_device(series, cw, cb, mw, mb, tv, tcol, sidx, smask, cot):
    n_graph = lax.axis_size("graph")
    n_tm = lax.axis_size("tm")
    steps, ch, sensors = series.shape
    tc = steps * ch
    slots = sidx.shape[2]
    halo = n_graph * slots
    wire = BF if slots % 16 == 0 else F32
    rounds = 4 * GATED_LAYERS
    scale = 1.0 / math.sqrt(float(steps * n_tm * sensors * n_graph))
    vm = pl.BlockSpec(memory_space=pltpu.VMEM)
    hb = pl.BlockSpec(memory_space=pltpu.HBM)
    cwt_shape = (*cw.shape[:2], cw.shape[3], cw.shape[2])
    ins = (
        series.reshape(tc, sensors),
        jnp.swapaxes(cw, 2, 3).reshape(-1, cw.shape[2]),
        cb,
        mw.reshape(-1, ch),
        mb,
        tv.reshape(-1, *tv.shape[2:]),
        tcol,
        sidx[0],
        smask[0],
        cot.reshape(tc, sensors),
    )
    er = 4 * ch // n_graph
    sm = pl.BlockSpec(memory_space=pltpu.SMEM)
    dma = pltpu.SemaphoreType.DMA
    out, gser, gconv, gmix = pl.pallas_call(
        functools.partial(kernel, n_graph, n_tm, steps, scale),
        out_shape=(
            jax.ShapeDtypeStruct((tc, sensors), BF),
            jax.ShapeDtypeStruct((tc, sensors), BF),
            jax.ShapeDtypeStruct(cwt_shape, F32),
            jax.ShapeDtypeStruct(mw.shape, F32),
        ),
        in_specs=[hb] * 6 + [sm] + [hb] * 3,
        out_specs=(vm,) * 4,
        scratch_shapes=[
            pltpu.VMEM((sensors, sensors), BF),
            pltpu.VMEM((sensors, sensors), BF),
            pltpu.VMEM((sensors, halo), BF),
            pltpu.VMEM((halo, sensors), BF),
            pltpu.VMEM((sensors, halo), BF),
            pltpu.VMEM((halo, sensors), BF),
            pltpu.VMEM((GATED_LAYERS, 2 * tc, 2 * tc), BF),
            pltpu.VMEM((GATED_LAYERS, tc, HOPS * tc), BF),
            pltpu.VMEM((GATED_LAYERS, sensors, 2 * tc), BF),
            pltpu.VMEM((GATED_LAYERS, sensors, HOPS * tc), BF),
            pltpu.VMEM((GATED_LAYERS, sensors, tc), F32),
            pltpu.VMEM((GATED_LAYERS, sensors, tc), F32),
            pltpu.VMEM((sensors, tc), F32),
            pltpu.VMEM((sensors, tc), F32),
            pltpu.VMEM((sensors, tc), F32),
            pltpu.VMEM((tc, sensors), BF),
            pltpu.VMEM((3, sensors // 2, tc), BF),
            pltpu.VMEM((3, sensors // 2, tc), BF),
            pltpu.VMEM((rounds, n_graph, 2, slots, tc), wire),
            pltpu.VMEM((rounds, n_graph, 2, slots, tc), wire),
            pltpu.VMEM((n_graph, er, tc), F32),
            pltpu.VMEM((n_tm, er, tc), F32),
            pltpu.VMEM((n_graph, ch, tc), F32),
            pltpu.VMEM((n_tm, ch, tc), F32),
            pltpu.VMEM((n_graph, er, tc), F32),
            pltpu.VMEM((n_graph, er, tc), F32),
            *[pltpu.VMEM(x.shape, x.dtype) for x in ins[:6] + ins[7:]],
            dma((9,)),
            dma((rounds, n_graph)), dma((rounds, n_graph)),
            dma((4,)), dma((4,)),
            dma((n_graph,)), dma((n_graph,)),
            dma((n_tm,)), dma((n_tm,)),
            dma((n_graph,)), dma((n_graph,)),
            dma((n_tm,)), dma((n_tm,)),
            dma((n_graph,)), dma((n_graph,)),
        ],
        compiler_params=pltpu.CompilerParams(
            collective_id=0, has_side_effects=True, vmem_limit_bytes=63 * 1024 * 1024
        ),
    )(*ins)
    results = (out, gser, gconv, gmix)
    out, gser, gconv, gmix = pl.pallas_call(
        store_kernel,
        out_shape=tuple(jax.ShapeDtypeStruct(x.shape, x.dtype) for x in results),
        in_specs=[vm] * 4,
        out_specs=(vm,) * 4,
    )(*results)
    gconv = jnp.swapaxes(gconv, 2, 3)
    return out.reshape(series.shape), gser.reshape(series.shape), gconv, gmix


def solution(mesh):
    return jax.shard_map(
        per_device,
        mesh=mesh,
        in_specs=(
            P("tm", None, "graph"),
            P(),
            P(),
            P(),
            P(),
            P("graph", None, None, None),
            P("graph", None),
            P("graph", None, None),
            P("graph", None, None),
            P("tm", None, "graph"),
        ),
        out_specs=(P("tm", None, "graph"), P("tm", None, "graph"), P(), P()),
        check_vma=False,
    )
```

```python
import functools
import math

import jax
import jax.numpy as jnp
from jax import lax
from jax.experimental import pallas as pl
from jax.experimental.pallas import tpu as pltpu
from jax.sharding import PartitionSpec as P

GATED_LAYERS = 2
HOPS = 5
BF = jnp.bfloat16
F32 = jnp.float32
MESH = pl.DeviceIdType.MESH


def dot(a, b):
    return lax.dot_general(a, b, (((1,), (0,)), ((), ())), preferred_element_type=F32)


def dot_nt(a, b):
    return lax.dot_general(a, b, (((1,), (1,)), ((), ())), preferred_element_type=F32)


def dot_tn(a, b):
    return lax.dot_general(a, b, (((0,), (0,)), ((), ())), preferred_element_type=F32)


def quot(x, n):
    return x >> (n.bit_length() - 1) if n & (n - 1) == 0 else x // n


def rest_of(x, n):
    return x & (n - 1) if n & (n - 1) == 0 else lax.rem(x, n)


def peers(count, body):
    if count <= 8:
        for off in range(count - 1, 0, -1):
            body(off)
    elif count > 1:
        lax.fori_loop(1, count, lambda off, c: (body(off), c)[1], 0)


def kernel(
    n_graph, n_tm, steps, scale,
    series_h, cw_h, cb_h, mw_h, mb_h, tv_h, tcol, sidx_h, smask_h, cot_h,
    out, gser, gconv, gmix,
    wl, wlt, wh, wht, gm, gmt, band, mixall, ext, hops, filt, gate, flow, ctr, hid_end,
    prev0, pack_s, pack_r, send, recv, e_buf, et_buf, l_buf, lt_buf,
    e_part, eg_buf, series, cw, cb, mw, mb, tv, sidx, smask, cot, in_sem,
    r_ssem, r_rsem, t_ssem, t_rsem, e_ssem, e_rsem, et_ssem, et_rsem,
    l_ssem, l_rsem, lt_ssem, lt_rsem, eg_ssem, eg_rsem,
):
    me = lax.axis_index("graph")
    z = lax.axis_index("tm")
    tc, sensors = series.shape
    ch = tc // steps
    half_s = sensors // 2
    slots = sidx.shape[1]
    halo = n_graph * slots
    tile = tv.shape[-1]
    rblocks, tslots = tcol.shape
    lblocks = sensors // tile
    hblocks = halo // tile
    wire = send.dtype

    def partner(off):
        if n_graph & (n_graph - 1) or n_graph > 8:
            return lax.rem(me + off, n_graph)
        p = 0
        bit = 1
        while bit < n_graph:
            p = p + lax.rem(me // bit + off // bit, 2) * bit
            bit *= 2
        return p

    er = e_part.shape[1]

    loads = [
        pltpu.make_async_copy(src, dst, in_sem.at[i])
        for i, (src, dst) in enumerate(
            ((cw_h, cw), (mw_h, mw), (cb_h, cb), (mb_h, mb), (tv_h, tv), (series_h, series),
             (sidx_h, sidx), (smask_h, smask), (cot_h, cot))
        )
    ]
    for load in loads:
        load.start()
    barrier = pltpu.get_barrier_semaphore()

    def greet_graph(off):
        pl.semaphore_signal(barrier, inc=1, device_id={"graph": partner(off)}, device_id_type=MESH)

    def greet_tm(off):
        pl.semaphore_signal(barrier, inc=1, device_id={"tm": lax.rem(z + off, n_tm)}, device_id_type=MESH)

    peers(n_graph, greet_graph)
    peers(n_tm, greet_tm)

    def shift_copy(slot, src, dst, by):
        return pltpu.make_async_remote_copy(
            src_ref=src, dst_ref=dst, send_sem=t_ssem.at[slot], recv_sem=t_rsem.at[slot],
            device_id={"tm": lax.rem(z + by + n_tm, n_tm)}, device_id_type=MESH,
        )

    up = z < n_tm - 1
    down = z > 0

    first = shift_copy(0, series_h.at[pl.ds(tc - ch, ch)], prev0.at[pl.ds(tc - ch, ch)], 1)
    prev0[pl.ds(0, tc - ch), :] = jnp.zeros((tc - ch, sensors), BF)

    row32 = lax.broadcasted_iota(jnp.int32, (ch, tc), 0)
    lane32 = lax.broadcasted_iota(jnp.int32, (ch, tc), 1)
    spread = jnp.where(rest_of(lane32, ch) == row32, 1.0, 0.0)
    spread_b = spread.astype(BF)
    rt = lax.broadcasted_iota(jnp.int32, (tc, tc), 0)
    lt = lax.broadcasted_iota(jnp.int32, (tc, tc), 1)
    rt, lt = quot(rt, ch), quot(lt, ch)
    same = rt == lt

    def before(d):
        return lt == rt - d

    def before_prev(d):
        return lt == rt - d + steps

    for load in loads[:4]:
        load.wait()
    taps = 2 * GATED_LAYERS
    rs = lax.broadcasted_iota(jnp.int32, (taps * ch, taps * tc), 0)
    ls = lax.broadcasted_iota(jnp.int32, (taps * ch, taps * tc), 1)
    spread_taps = jnp.where(quot(ls, tc) * ch + rest_of(ls, ch) == rs, 1.0, 0.0).astype(BF)
    def after(d):
        return rt == lt - d

    def after_prev(d):
        return rt == lt - d + steps

    cwr = dot_tn(cw[...], spread_taps)
    mwr = dot(mw[...], spread_b)

    def stack(x, base):
        return jnp.concatenate([x[base:base + ch]] * steps, axis=0)

    for l in range(GATED_LAYERS):
        d = l + 1
        for h in range(2):
            w0 = stack(cwr[:, (l * 2) * tc:(l * 2 + 1) * tc], h * ch)
            w1 = stack(cwr[:, (l * 2 + 1) * tc:(l * 2 + 2) * tc], h * ch)
            own = jnp.where(same, w0, 0.0) + jnp.where(before(d), w1, 0.0)
            band[l, pl.ds(h * tc, tc), pl.ds(0, tc)] = own.astype(BF)
            band[l, pl.ds(h * tc, tc), pl.ds(tc, tc)] = jnp.where(before_prev(d), w1, 0.0).astype(BF)
        for k in range(HOPS):
            mk = stack(mwr, (l * HOPS + k) * ch)
            mixall[l, :, pl.ds(k * tc, tc)] = jnp.where(same, mk, 0.0).astype(BF)

    r64 = lax.broadcasted_iota(jnp.int32, (2 * ch, 2 * tc), 0)
    l64 = lax.broadcasted_iota(jnp.int32, (2 * ch, 2 * tc), 1)
    spread2 = jnp.where(rest_of(l64, ch) + quot(l64, tc) * ch == r64, 1.0, 0.0)
    cbias = lax.dot_general(cb[...], spread2, (((1,), (0,)), ((), ())), precision=lax.Precision.HIGHEST, preferred_element_type=F32)
    mbias = lax.dot_general(mb[...], spread, (((1,), (0,)), ((), ())), precision=lax.Precision.HIGHEST, preferred_element_type=F32)

    pl.semaphore_wait(barrier, n_graph - 1 + n_tm - 1)

    @pl.when(up)
    def _():
        first.start()

    for load in loads[4:]:
        load.wait()
    for r in range(rblocks):
        tiles = [tv[r * tslots + k].astype(F32) for k in range(tslots)]
        flips = [t.T for t in tiles]
        for c in range(lblocks + hblocks):
            a = jnp.zeros((tile, tile), F32)
            b = jnp.zeros((tile, tile), F32)
            for k in range(tslots):
                on = (tcol[r, k] == c).astype(jnp.int32).astype(F32)
                a = a + tiles[k] * on
                b = b + flips[k] * on
            a = a.astype(BF)
            b = b.astype(BF)
            if c < lblocks:
                wl[pl.ds(r * tile, tile), pl.ds(c * tile, tile)] = a
                wlt[pl.ds(c * tile, tile), pl.ds(r * tile, tile)] = b
            else:
                ch_at = c - lblocks
                wh[pl.ds(r * tile, tile), pl.ds(ch_at * tile, tile)] = a
                wht[pl.ds(ch_at * tile, tile), pl.ds(r * tile, tile)] = b

    key = jnp.where(smask[...] != 0, sidx[...] + 1, 0)
    es = lax.broadcasted_iota(jnp.int32, (slots, halo), 0)
    ej = lax.broadcasted_iota(jnp.int32, (slots, halo), 1)
    pick = jnp.where(rest_of(ej, slots) == es, 1.0, 0.0).astype(BF)
    hi = dot((key >> 5).astype(F32).astype(BF), pick)
    lo = dot((key & 31).astype(F32).astype(BF), pick)
    pr = lax.broadcasted_iota(jnp.int32, (n_graph, halo), 0)
    pj = quot(lax.broadcasted_iota(jnp.int32, (n_graph, halo), 1), slots)
    keys = jnp.sum(jnp.where(pr == pj, hi * 32.0 + lo, 0.0), axis=0, keepdims=True)
    ids = lax.broadcasted_iota(jnp.int32, (sensors, halo), 0).astype(F32) + 1.0
    onehot = jnp.where(ids == keys, 1.0, 0.0)
    gm[...] = onehot.astype(BF)
    gmt[...] = onehot.T.astype(BF)

    ext[0, :, pl.ds(0, tc)] = series[...].astype(F32).T.astype(BF)

    def graph_copy(src, dst, ssem, rsem, p):
        return pltpu.make_async_remote_copy(
            src_ref=src, dst_ref=dst, send_sem=ssem, recv_sem=rsem,
            device_id={"graph": p}, device_id_type=MESH,
        )

    def tm_copy(src, dst, ssem, rsem, p):
        return pltpu.make_async_remote_copy(
            src_ref=src, dst_ref=dst, send_sem=ssem, recv_sem=rsem,
            device_id={"tm": p}, device_id_type=MESH,
        )

    def pair(r, pull_in, push_in, filler):
        sp = dot(gmt[...], pull_in)
        sb = dot(wht[...], push_in).astype(BF).astype(F32)
        send[r, :, 0] = sp.reshape(n_graph, slots, tc).astype(wire)
        send[r, :, 1] = sb.reshape(n_graph, slots, tc).astype(wire)

        def go(off):
            p = partner(off)
            graph_copy(send.at[r, p], recv.at[r, me], r_ssem.at[r, p], r_rsem.at[r], p).start()

        peers(n_graph, go)
        recv[r, me] = send[r, me]
        pulled = dot(wl[...], pull_in)
        pushed = dot(wlt[...], push_in)
        filler()

        arrived = recv.at[r, pl.ds(0, n_graph - 1)]
        graph_copy(arrived, arrived, r_ssem.at[r, 0], r_rsem.at[r], partner(1)).wait_recv()
        rp = recv[r, :, 0].reshape(halo, tc).astype(BF)
        rb = recv[r, :, 1].reshape(halo, tc).astype(BF)
        return pulled + dot(wh[...], rp), pushed + dot(gm[...], rb)

    lane_half = lax.broadcasted_iota(jnp.int32, (half_s, tc), 1) < tc // 2

    def pack(x):
        return jnp.where(lane_half, pltpu.roll(x[:half_s], tc // 2, 1), x[half_s:]).astype(BF)

    def unpack(p):
        x = p.astype(F32)
        return jnp.concatenate([pltpu.roll(x, tc // 2, 1), x], axis=0)

    def take_cotangent():
        ctr[...] = cot[...].astype(F32).T

    for l in range(GATED_LAYERS):
        if l == 0:
            @pl.when(down)
            def _():
                first.wait_recv()

            @pl.when(jnp.logical_not(down))
            def _():
                prev0[pl.ds(tc - ch, ch), :] = jnp.zeros((ch, sensors), BF)

            ext[0, :, pl.ds(tc, tc)] = prev0[...].astype(F32).T.astype(BF)
            pre = dot_nt(ext[0], band[0])
        else:
            pre_own = dot_nt(ext[l, :, pl.ds(0, tc)], band[l, :, pl.ds(0, tc)])

            @pl.when(down)
            def _():
                shift_copy(1, pack_s.at[0], pack_r.at[0], 1).wait_recv()

            @pl.when(jnp.logical_not(down))
            def _():
                pack_r[0] = jnp.zeros((half_s, tc), BF)

            ext[l, :, pl.ds(tc, tc)] = unpack(pack_r[0]).astype(BF)
            pre = pre_own + dot_nt(ext[l, :, pl.ds(tc, tc)], band[l, :, pl.ds(tc, tc)])
        pre = pre + cbias[l:l + 1]
        f = jnp.tanh(pre[:, :tc])
        g = jax.nn.sigmoid(pre[:, tc:])
        filt[l] = f
        gate[l] = g
        gated = (f * g).astype(BF)
        hops[l, :, pl.ds(0, tc)] = gated
        fo, bo = pair(2 * l, gated, gated, take_cotangent if l == 0 else (lambda: None))
        fo = fo.astype(BF)
        bo = bo.astype(BF)
        hops[l, :, pl.ds(tc, tc)] = fo
        hops[l, :, pl.ds(3 * tc, tc)] = bo
        part = []

        def mix_early():
            m = dot_nt(hops[l, :, pl.ds(0, 2 * tc)], mixall[l, :, pl.ds(0, 2 * tc)])
            part.append(m + dot_nt(hops[l, :, pl.ds(3 * tc, tc)], mixall[l, :, pl.ds(3 * tc, tc)]))

        f2, b2 = pair(2 * l + 1, fo, bo, mix_early)
        f2 = f2.astype(BF)
        b2 = b2.astype(BF)
        hops[l, :, pl.ds(2 * tc, tc)] = f2
        hops[l, :, pl.ds(4 * tc, tc)] = b2
        mixed = part[0] + dot_nt(f2, mixall[l, :, pl.ds(2 * tc, tc)]) + dot_nt(b2, mixall[l, :, pl.ds(4 * tc, tc)])
        mixed = mixed + mbias[l:l + 1]
        hid = ext[l, :, pl.ds(0, tc)].astype(F32) + mixed
        if l + 1 < GATED_LAYERS:
            pack_s[0] = pack(hid)

            @pl.when(up)
            def _():
                shift_copy(1, pack_s.at[0], pack_r.at[0], 1).start()

            ext[l + 1, :, pl.ds(0, tc)] = hid.astype(BF)
        else:
            hid_end[...] = hid

    flow[...] = ctr[...]

    lane_g = quot(lax.broadcasted_iota(jnp.int32, (ch, tc), 1), ch)

    def fold(x):
        y = x[0:ch]
        for t in range(1, steps):
            y = y + x[t * ch:(t + 1) * ch]
        sh = ch
        while sh < tc:
            y = y + pltpu.roll(y, sh, 1)
            sh *= 2
        return y

    def lanes_of(xs):
        y = jnp.zeros((ch, tc), F32)
        for g, x in enumerate(xs):
            y = jnp.where(lane_g == g, x, y)
        return y

    e_conv = None
    e_mix = [None, None]

    def gather_start(buf, ssem, rsem, count, here, copy):
        def go(off):
            p = lax.rem(here + off, count)
            copy(buf.at[here], buf.at[here], ssem.at[p], rsem.at[here], p).start()

        peers(count, go)

    def gather_sum(buf, ssem, rsem, count, here, copy):
        def take(off):
            p = lax.rem(here + off, count)
            copy(buf.at[p], buf.at[p], ssem.at[p], rsem.at[p], p).wait_recv()

        peers(count, take)
        total = buf[0]
        for p in range(1, count):
            total = total + buf[p]
        return total

    for l in reversed(range(GATED_LAYERS)):
        d = l + 1
        fr = flow[...].astype(BF)
        r0 = 2 * GATED_LAYERS + 2 * (GATED_LAYERS - 1 - l)

        def back(k):
            return dot(fr, mixall[l, :, pl.ds(k * tc, tc)])

        rest = []

        def fill_one():
            rest.extend([back(0), back(1), back(3)])
            prod = dot_tn(fr, hops[l])
            folds = [fold(jnp.where(same, prod[:, k * tc:(k + 1) * tc], 0.0)) for k in range(HOPS)]
            if l == GATED_LAYERS - 1:
                out[...] = hid_end[...].T.astype(BF)
            e_mix[l] = (lanes_of(folds[:4]), folds[4])
            if l == 0:
                early = jnp.concatenate(
                    [e_conv, e_mix[1][0], e_mix[0][0], lanes_of([e_mix[1][1], e_mix[0][1]])], axis=0
                )
                for p in range(n_graph):
                    e_part[p] = early[p * er:(p + 1) * er]

                def scatter(off):
                    p = partner(off)
                    graph_copy(e_part.at[p], e_buf.at[me], e_ssem.at[p], e_rsem.at[me], p).start()

                peers(n_graph, scatter)
                e_buf[me] = e_part[me]

        bi, fi = pair(r0, back(4).astype(BF), back(2).astype(BF), fill_one)

        def fill_two():
            if l == 0:
                et_buf[z] = gather_sum(e_buf, e_ssem, e_rsem, n_graph, me, graph_copy)
                gather_start(et_buf, et_ssem, et_rsem, n_tm, z, tm_copy)

        bo, fo = pair(r0 + 1, (rest[2] + bi).astype(BF), (rest[1] + fi).astype(BF), fill_two)
        gg = rest[0] + fo + bo
        f = filt[l]
        g = gate[l]
        gf = gg * g * (1.0 - f * f)
        gt = gg * f * g * (1.0 - g)
        gp = jnp.concatenate([gf, gt], axis=1).astype(BF)
        slot = 2 + (GATED_LAYERS - 1 - l)
        at = 1 + (GATED_LAYERS - 1 - l)
        pack_s[at] = pack(dot(gp, band[l, :, pl.ds(tc, tc)]))

        @pl.when(down)
        def _():
            shift_copy(slot, pack_s.at[at], pack_r.at[at], -1).start()

        prod = dot_tn(ext[l], gp)
        pieces = []
        for tap in range(2):
            for h in range(2):
                own = prod[:tc, h * tc:(h + 1) * tc]
                if tap == 0:
                    x = jnp.where(same, own, 0.0)
                else:
                    x = jnp.where(after(d), own, 0.0) + jnp.where(after_prev(d), prod[tc:, h * tc:(h + 1) * tc], 0.0)
                pieces.append(fold(x))
        conv = lanes_of(pieces)
        if l == 0:
            l_buf[me] = conv
            gather_start(l_buf, l_ssem, l_rsem, n_graph, me, graph_copy)
            eg_buf[me] = gather_sum(et_buf, et_ssem, et_rsem, n_tm, z, tm_copy)
            gather_start(eg_buf, eg_ssem, eg_rsem, n_graph, me, graph_copy)
        else:
            e_conv = conv
        new = flow[...] + dot(gp, band[l, :, pl.ds(0, tc)])

        @pl.when(up)
        def _():
            shift_copy(slot, pack_s.at[at], pack_r.at[at], -1).wait_recv()

        @pl.when(jnp.logical_not(up))
        def _():
            pack_r[at] = jnp.zeros((half_s, tc), BF)

        lanes = lax.broadcasted_iota(jnp.int32, (sensors, tc), 1)
        flow[...] = new + jnp.where(lanes >= tc // 2, unpack(pack_r[at]), 0.0)

    lt_buf[z] = gather_sum(l_buf, l_ssem, l_rsem, n_graph, me, graph_copy)
    gather_start(lt_buf, lt_ssem, lt_rsem, n_tm, z, tm_copy)
    gser[...] = flow[...].T.astype(BF)

    def lane_group(x, g):
        return (pltpu.roll(x, tc - g * ch, 1) if g else x)[:, :ch]

    def put_conv(l, x):
        gconv[l, 0] = x[:, :2 * ch]
        gconv[l, 1] = pltpu.roll(x, tc - 2 * ch, 1)[:, :2 * ch]

    def take_group(off):
        p = partner(off)
        graph_copy(eg_buf.at[p], eg_buf.at[p], eg_ssem.at[p], eg_rsem.at[p], p).wait_recv()

    peers(n_graph, take_group)
    e = jnp.concatenate([eg_buf[p] for p in range(n_graph)], axis=0) * scale
    put_conv(1, e[:ch])
    for k in range(4):
        gmix[1, k] = lane_group(e[ch:2 * ch], k)
        gmix[0, k] = lane_group(e[2 * ch:3 * ch], k)
    gmix[1, 4] = lane_group(e[3 * ch:], 0)
    gmix[0, 4] = lane_group(e[3 * ch:], 1)
    put_conv(0, gather_sum(lt_buf, lt_ssem, lt_rsem, n_tm, z, tm_copy) * scale)

    def sent_graph(off):
        p = partner(off)
        for r in range(4 * GATED_LAYERS):
            graph_copy(send.at[r, p], recv.at[r, me], r_ssem.at[r, p], r_rsem.at[r], p).wait_send()
        graph_copy(e_part.at[p], e_buf.at[me], e_ssem.at[p], e_rsem.at[me], p).wait_send()
        graph_copy(eg_buf.at[me], eg_buf.at[me], eg_ssem.at[p], eg_rsem.at[me], p).wait_send()
        graph_copy(l_buf.at[me], l_buf.at[me], l_ssem.at[p], l_rsem.at[me], p).wait_send()

    peers(n_graph, sent_graph)

    def sent_tm(off):
        p = lax.rem(z + off, n_tm)
        tm_copy(et_buf.at[z], et_buf.at[z], et_ssem.at[p], et_rsem.at[z], p).wait_send()
        tm_copy(lt_buf.at[z], lt_buf.at[z], lt_ssem.at[p], lt_rsem.at[z], p).wait_send()

    peers(n_tm, sent_tm)

    @pl.when(up)
    def _():
        first.wait_send()
        shift_copy(1, pack_s.at[0], pack_r.at[0], 1).wait_send()

    @pl.when(down)
    def _():
        shift_copy(2, pack_s.at[1], pack_r.at[1], -1).wait_send()
        shift_copy(3, pack_s.at[2], pack_r.at[2], -1).wait_send()


def store_kernel(a, b, c, d, ao, bo, co, do):
    ao[...] = a[...]
    bo[...] = b[...]
    co[...] = c[...]
    do[...] = d[...]


def per_device(series, cw, cb, mw, mb, tv, tcol, sidx, smask, cot):
    n_graph = lax.axis_size("graph")
    n_tm = lax.axis_size("tm")
    steps, ch, sensors = series.shape
    tc = steps * ch
    slots = sidx.shape[2]
    halo = n_graph * slots
    wire = BF if slots % 16 == 0 else F32
    rounds = 4 * GATED_LAYERS
    scale = 1.0 / math.sqrt(float(steps * n_tm * sensors * n_graph))
    vm = pl.BlockSpec(memory_space=pltpu.VMEM)
    hb = pl.BlockSpec(memory_space=pltpu.HBM)
    cwt_shape = (*cw.shape[:2], cw.shape[3], cw.shape[2])
    ins = (
        series.reshape(tc, sensors),
        jnp.swapaxes(cw, 2, 3).reshape(-1, cw.shape[2]),
        cb,
        mw.reshape(-1, ch),
        mb,
        tv.reshape(-1, *tv.shape[2:]),
        tcol,
        sidx[0],
        smask[0],
        cot.reshape(tc, sensors),
    )
    er = 4 * ch // n_graph
    sm = pl.BlockSpec(memory_space=pltpu.SMEM)
    dma = pltpu.SemaphoreType.DMA
    out, gser, gconv, gmix = pl.pallas_call(
        functools.partial(kernel, n_graph, n_tm, steps, scale),
        out_shape=(
            jax.ShapeDtypeStruct((tc, sensors), BF),
            jax.ShapeDtypeStruct((tc, sensors), BF),
            jax.ShapeDtypeStruct(cwt_shape, F32),
            jax.ShapeDtypeStruct(mw.shape, F32),
        ),
        in_specs=[hb] * 6 + [sm] + [hb] * 3,
        out_specs=(vm,) * 4,
        scratch_shapes=[
            pltpu.VMEM((sensors, sensors), BF),
            pltpu.VMEM((sensors, sensors), BF),
            pltpu.VMEM((sensors, halo), BF),
            pltpu.VMEM((halo, sensors), BF),
            pltpu.VMEM((sensors, halo), BF),
            pltpu.VMEM((halo, sensors), BF),
            pltpu.VMEM((GATED_LAYERS, 2 * tc, 2 * tc), BF),
            pltpu.VMEM((GATED_LAYERS, tc, HOPS * tc), BF),
            pltpu.VMEM((GATED_LAYERS, sensors, 2 * tc), BF),
            pltpu.VMEM((GATED_LAYERS, sensors, HOPS * tc), BF),
            pltpu.VMEM((GATED_LAYERS, sensors, tc), F32),
            pltpu.VMEM((GATED_LAYERS, sensors, tc), F32),
            pltpu.VMEM((sensors, tc), F32),
            pltpu.VMEM((sensors, tc), F32),
            pltpu.VMEM((sensors, tc), F32),
            pltpu.VMEM((tc, sensors), BF),
            pltpu.VMEM((3, sensors // 2, tc), BF),
            pltpu.VMEM((3, sensors // 2, tc), BF),
            pltpu.VMEM((rounds, n_graph, 2, slots, tc), wire),
            pltpu.VMEM((rounds, n_graph, 2, slots, tc), wire),
            pltpu.VMEM((n_graph, er, tc), F32),
            pltpu.VMEM((n_tm, er, tc), F32),
            pltpu.VMEM((n_graph, ch, tc), F32),
            pltpu.VMEM((n_tm, ch, tc), F32),
            pltpu.VMEM((n_graph, er, tc), F32),
            pltpu.VMEM((n_graph, er, tc), F32),
            *[pltpu.VMEM(x.shape, x.dtype) for x in ins[:6] + ins[7:]],
            dma((9,)),
            dma((rounds, n_graph)), dma((rounds,)),
            dma((4,)), dma((4,)),
            dma((n_graph,)), dma((n_graph,)),
            dma((n_tm,)), dma((n_tm,)),
            dma((n_graph,)), dma((n_graph,)),
            dma((n_tm,)), dma((n_tm,)),
            dma((n_graph,)), dma((n_graph,)),
        ],
        compiler_params=pltpu.CompilerParams(
            collective_id=0, has_side_effects=True, vmem_limit_bytes=63 * 1024 * 1024
        ),
    )(*ins)
    results = (out, gser, gconv, gmix)
    out, gser, gconv, gmix = pl.pallas_call(
        store_kernel,
        out_shape=tuple(jax.ShapeDtypeStruct(x.shape, x.dtype) for x in results),
        in_specs=[vm] * 4,
        out_specs=(vm,) * 4,
    )(*results)
    gconv = jnp.swapaxes(gconv, 2, 3)
    return out.reshape(series.shape), gser.reshape(series.shape), gconv, gmix


def solution(mesh):
    return jax.shard_map(
        per_device,
        mesh=mesh,
        in_specs=(
            P("tm", None, "graph"),
            P(),
            P(),
            P(),
            P(),
            P("graph", None, None, None),
            P("graph", None),
            P("graph", None, None),
            P("graph", None, None),
            P("tm", None, "graph"),
        ),
        out_specs=(P("tm", None, "graph"), P("tm", None, "graph"), P(), P()),
        check_vma=False,
    )
```
